256 devices in a mesh: blk: 128 (over z, y_hi, x, core), feat: 2 (over y_lo).
Axes of the slice: x: 4, y: 4 (y_hi: 2, y_lo: 2; y = y_hi * 2 + y_lo), z: 8, core: 2. Of those that a mesh axis runs over, the one named last changes fastest.
Arguments:
- features: bfloat16 [65536, 1024], P('blk', 'feat'), may hold values from -24 to 24
- weight_in: bfloat16 [1024, 1024], P(None, 'feat'), may hold values from -0.1875 to 0.1875
- weight_out: bfloat16 [1024, 1024], P(None, 'feat'), may hold values from -0.1875 to 0.1875
- adj_tiles: bfloat16 [128, 5, 8, 128, 128], P('blk'), may hold values from -0.625 to 0.625
- tile_rows: int32 [128, 5, 8], P('blk'), may hold values from 0 to 3, as said below
- tile_cols: int32 [128, 5, 8], P('blk'), may hold values from 0 to 3, as said below
- tile_counts: int32 [128, 5], P('blk'), may hold values from 0 to 8
- cotangent: bfloat16 [65536, 1024], P('blk', 'feat'), may hold values from -0.0625 to 0.0625
Outputs:
- layer_output: bfloat16 [65536, 1024], P('blk', 'feat')
- grad_weight_in: float32 [1024, 1024], P('blk', 'feat')
- grad_weight_out: float32 [1024, 1024], P('blk', 'feat')
The draws below stay inside these ranges and needn't reach their ends.
Inputs may be any that keep to these rules, and one draw needn't show every extreme that they name: `tile_rows`: within one block and cycle step the 8 slots name distinct (row, column) tile pairs. `tile_cols`: within one block and cycle step the 8 slots name distinct (row, column) tile pairs.
All inputs are finite; a program needn't handle non-finite values.
Results may differ from the reference program's by a relative error of at most 0.0064.
Values may be sent and summed in bfloat16 or wider, within the bound.
A program may use at most 128 MiB of HBM per device.

```python
import jax
import jax.numpy as jnp
from jax import lax

FEAT = 1024
HIDDEN_SIZE = 1024
TILE = 128
RADIUS = 2
CAP = 8
ROWS_DEV = 512
STEPS = 5
TILE_ROWS = 4
NBLOCKS = 128
NODES = 65536


def index_pairs(key):
    key_list = jax.random.split(jax.random.fold_in(key, 11), NBLOCKS * STEPS)

    def one_order(one_key):
        return jax.random.permutation(one_key, TILE_ROWS * TILE_ROWS)
    orders = jax.vmap(one_order)(key_list)
    return orders[:, :CAP].reshape(NBLOCKS, STEPS, CAP).astype(jnp.int32)


def draw_tile_rows(key, part):
    return (index_pairs(key) // TILE_ROWS).astype(jnp.int32)


def draw_tile_cols(key, part):
    return (index_pairs(key) % TILE_ROWS).astype(jnp.int32)


def draw_tile_counts(key, part):
    first_draw = jax.random.randint(jax.random.fold_in(key, 21), (NBLOCKS, STEPS), 0, CAP + 1)
    second_draw = jax.random.randint(jax.random.fold_in(key, 22), (NBLOCKS, STEPS), 0, CAP + 1)
    skewed = first_draw * second_draw // CAP
    centre = (jnp.arange(STEPS) == RADIUS)[None, :]
    return jnp.where(centre, CAP, skewed).astype(jnp.int32)


def spiked(array, rng, source, target, parts, factor):
    def block_of(dim):
        return (jnp.arange(array.shape[dim]) // (array.shape[dim] // parts)).reshape((-1,) + (1,) * (array.ndim - 1 - dim))

    near = jax.random.permutation(rng, parts)[block_of(target)]
    far = (block_of(target) + parts // 2) % parts
    return jnp.where((block_of(source) == near) | (block_of(source) == far), factor * array, array)


def steps_of(own_key, extent, cuts, smallest, high):
    level, own = 1.0, jax.random.fold_in(own_key, 6)
    for position, parts in cuts:
        heights = jnp.exp(jax.random.uniform(jax.random.fold_in(own, position), (parts,), jnp.float32, smallest / len(cuts), high / len(cuts)))
        level = level * jnp.repeat(heights, extent[position] // parts).reshape([-1 if axis == position else 1 for axis in range(len(extent))])
    return level


def noise(rng, extent, width, limit, shards=(), kind=jnp.bfloat16):
    values = jax.random.normal(rng, extent, jnp.float32) * width
    if len(shards) > 0:
        values = steps_of(rng, extent, shards, -0.22, 0.18) * values
    return jnp.clip(values, min=-limit, max=limit).astype(kind)


def noise_with(key, shape, scale, reach, cuts, heavy, held_as=jnp.bfloat16):
    array = scale * jax.random.normal(key, shape, jnp.float32)
    if cuts:
        array = array * steps_of(key, shape, cuts, -0.22, 0.18)
    return jnp.clip(spiked(array, jax.random.fold_in(key, 3), *heavy), -reach, reach).astype(held_as)


def setup_inputs(seed: int = 0) -> dict:
    keys = jax.random.split(jax.random.key(seed), 9)
    features = noise_with(keys[0], (NODES, FEAT), 1.0, 24.0, ((0, 128), (1, 2)), (0, 1, 128, 5.5))
    weight_in = noise(keys[1], (FEAT, HIDDEN_SIZE), FEAT ** -0.5, 0.1875, ((1, 2),))
    weight_out = noise(keys[2], (HIDDEN_SIZE, HIDDEN_SIZE), HIDDEN_SIZE ** -0.5, 0.1875, ((1, 2),))
    adj_tiles = noise(keys[3], (NBLOCKS, STEPS, CAP, TILE, TILE), ((TILE * (CAP // TILE_ROWS + 2)) ** -0.5), 0.625, ((0, 128),))
    tile_rows = draw_tile_rows(jax.random.fold_in(keys[8], 71), 0)
    tile_cols = draw_tile_cols(jax.random.fold_in(keys[8], 71), 0)
    tile_counts = draw_tile_counts(jax.random.fold_in(keys[8], 71), 0)
    cotangent = noise(keys[7], (NODES, HIDDEN_SIZE), (NODES ** -0.5), 0.0625, ((0, 128), (1, 2)))
    return {"features": features, "weight_in": weight_in, "weight_out": weight_out, "adj_tiles": adj_tiles, "tile_rows": tile_rows, "tile_cols": tile_cols, "tile_counts": tile_counts, "cotangent": cotangent}


def slot_weights(put_ids, live_count, block_rows):
    chosen = put_ids[:, None] == jnp.arange(block_rows, dtype=jnp.int32)[None, :]
    live_mask = (jnp.arange(put_ids.shape[0], dtype=jnp.int32) < live_count)[:, None]
    return (chosen & live_mask).astype(jnp.float32)


def spread_rows(adj_tiles, tile_rows, tile_cols, tile_counts, values_in):
    columns = values_in.shape[1]
    blocks = values_in.reshape(NBLOCKS, TILE_ROWS, TILE, columns)

    def one_block(block_index):
        summed = jnp.zeros((TILE_ROWS, TILE, columns), jnp.float32)
        for cycle_step in range(STEPS):
            source = (block_index + cycle_step - RADIUS) % NBLOCKS
            source_rows = lax.dynamic_index_in_dim(blocks, source, 0, keepdims=False)
            picked = jnp.take(source_rows, tile_cols[block_index, cycle_step], axis=0)
            product = jnp.einsum("kab,kbw->kaw", adj_tiles[block_index, cycle_step].astype(jnp.float32),
                                 picked.astype(jnp.float32), precision=lax.Precision.HIGHEST)
            weights = slot_weights(tile_rows[block_index, cycle_step], tile_counts[block_index, cycle_step], TILE_ROWS)
            summed = summed + jnp.einsum("kr,kaw->raw", weights, product, precision=lax.Precision.HIGHEST)
        return summed.reshape(ROWS_DEV, columns)

    return lax.map(one_block, jnp.arange(NBLOCKS, dtype=jnp.int32)).reshape(NODES, columns)


def return_rows(adj_tiles, tile_rows, tile_cols, tile_counts, values_in):
    columns = values_in.shape[1]
    blocks = values_in.reshape(NBLOCKS, TILE_ROWS, TILE, columns)

    def one_block(block_index):
        summed = jnp.zeros((TILE_ROWS, TILE, columns), jnp.float32)
        for cycle_step in range(STEPS):
            source = (block_index - (cycle_step - RADIUS)) % NBLOCKS
            source_rows = lax.dynamic_index_in_dim(blocks, source, 0, keepdims=False)
            picked = jnp.take(source_rows, tile_rows[source, cycle_step], axis=0)
            product = jnp.einsum("kba,kbw->kaw", adj_tiles[source, cycle_step].astype(jnp.float32),
                                 picked.astype(jnp.float32), precision=lax.Precision.HIGHEST)
            weights = slot_weights(tile_cols[source, cycle_step], tile_counts[source, cycle_step], TILE_ROWS)
            summed = summed + jnp.einsum("kr,kaw->raw", weights, product, precision=lax.Precision.HIGHEST)
        return summed.reshape(ROWS_DEV, columns)

    return lax.map(one_block, jnp.arange(NBLOCKS, dtype=jnp.int32)).reshape(NODES, columns)


def reference(features, weight_in, weight_out, adj_tiles, tile_rows, tile_cols, tile_counts, cotangent):
    spread_in = spread_rows(adj_tiles, tile_rows, tile_cols, tile_counts, features).astype(jnp.bfloat16)
    pre_hidden = jnp.dot(spread_in, weight_in, preferred_element_type=jnp.float32)
    hidden = jax.nn.silu(pre_hidden).astype(jnp.bfloat16)
    spread_hidden = spread_rows(adj_tiles, tile_rows, tile_cols, tile_counts, hidden).astype(jnp.bfloat16)
    layer_output = jnp.dot(spread_hidden, weight_out, preferred_element_type=jnp.float32).astype(jnp.bfloat16)
    back_mixed = lax.dot_general(cotangent, weight_out, (((1,), (1,)), ((), ())),
                                 preferred_element_type=jnp.float32).astype(jnp.bfloat16)
    back_hidden = return_rows(adj_tiles, tile_rows, tile_cols, tile_counts, back_mixed)
    sigmoid_gate = jax.nn.sigmoid(pre_hidden)
    back_pre = (back_hidden * sigmoid_gate * (1.0 + pre_hidden * (1.0 - sigmoid_gate))).astype(jnp.bfloat16)
    grad_weight_in = lax.dot_general(spread_in, back_pre, (((0,), (0,)), ((), ())),
                                     preferred_element_type=jnp.float32)
    grad_weight_out = lax.dot_general(spread_hidden, cotangent, (((0,), (0,)), ((), ())),
                                      preferred_element_type=jnp.float32)
    return (layer_output, grad_weight_in, grad_weight_out)
```

```python
import functools

import jax
import jax.numpy as jnp
from jax import lax
from jax.experimental import pallas as pl
from jax.experimental.pallas import tpu as pltpu
from jax.sharding import PartitionSpec as P

F32 = jnp.float32
BF = jnp.bfloat16
MESH = pl.DeviceIdType.MESH
NB = 128
NZ, NY, NX, NC = 8, 2, 4, 2
N = 512
W = 512
TILE = 128
OFFS = (1, -1, 2, -2)
XCH = 2
XW = W // XCH
RCH = 2
RW = N // RCH
SUB = 256


def dot(a, b):
    return jnp.dot(a, b, preferred_element_type=F32)


def dot_tn(a, b):
    return lax.dot_general(a, b, (((0,), (0,)), ((), ())), preferred_element_type=F32)


def dot_nt(a, b):
    return lax.dot_general(a, b, (((1,), (1,)), ((), ())), preferred_element_type=F32)


def fold(v):
    return jnp.concatenate([v[..., : W // 2], v[..., W // 2 :]], axis=-2)


def loop(count, body):
    def step(i, carry):
        body(i)
        return carry

    lax.fori_loop(0, count, step, 0)


def span(i, size):
    return pl.ds(pl.multiple_of(i * size, size), size)


class Sems:
    def __init__(self, send, recv):
        self.send, self.recv, self.used = send, recv, 0

    def copy(self, src, dst, device):
        i = self.used
        self.used += 1
        made = pltpu.make_async_remote_copy(
            src_ref=src,
            dst_ref=dst,
            send_sem=self.send.at[i],
            recv_sem=self.recv.at[i],
            device_id=device,
            device_id_type=MESH,
        )
        made.start()
        return made


NREMOTE = 80


def kernel(
    x_h, win_h, wout_h, tiles_h, rows, cols, cnts, cot_h,
    out_o, gin_o, gout_o,
    x, win, wout, tiles, cot,
    a, xg, sacc, sfull, pre, hfull, dact, zacc, z, zg,
    pbuf, pr, cacc, cp, bhs, bhr, bp, oacc,
    g1, g1c, g1r1, g1x, g1r2f, g1r2, g1y, g1r3f, g1r3, g1z,
    g2, g2c, g2r1, g2z, g2r2f, g2r2, g2x, g2r3f, g2r3, g2y,
    lsem, ssem, rsem,
):
    b = lax.axis_index("blk")
    f = lax.axis_index("feat")
    c = lax.rem(b, NC)
    ix = lax.rem(b // NC, NX)
    iy = lax.rem(b // (NC * NX), NY)
    iz = b // (NC * NX * NY)
    nf = 1 - f
    nc = 1 - c

    def node(zz, yy, xx, cc):
        return (((zz * NY + yy) * NX + xx) * NC + cc, f)

    def near(o):
        return (lax.rem(b + o + NB, NB), f)

    peer = (b, nf)
    partner = node(iz, iy, ix, nc)
    xpeers = [lax.rem(ix + d, NX) for d in range(1, NX)]
    zpeers = [lax.rem(iz + d, NZ) for d in range(1, NZ)]
    ypeer = 1 - iy

    greeted = [near(o) for o in OFFS] + [peer, partner]
    greeted += [node(iz, iy, xx, c) for xx in xpeers]
    greeted += [node(zz, iy, ix, c) for zz in zpeers]
    greeted += [node(iz, ypeer, ix, c)]
    barrier = pltpu.get_barrier_semaphore()
    for device in greeted:
        pl.semaphore_signal(barrier, inc=1, device_id=device, device_id_type=MESH)
    loads = []
    for i, (src, dst) in enumerate(
        ((x_h, x), (tiles_h, tiles), (cot_h, cot), (win_h, win), (wout_h, wout))
    ):
        made = pltpu.make_async_copy(src, dst, lsem.at[i])
        made.start()
        loads.append(made)
    loads[0].wait()
    pl.semaphore_wait(barrier, len(greeted))

    sems = Sems(ssem, rsem)
    xcopies = []
    for j in range(XCH):
        cs = pl.ds(j * XW, XW)
        xcopies.append(
            [sems.copy(x.at[:, cs], xg.at[i, :, cs], near(-o)) for i, o in enumerate(OFFS)]
        )

    loads[1].wait()

    def densify(s):
        live = cnts[0, s]
        place = [
            jnp.where(k < live, rows[0, s, k] * 4 + cols[0, s, k], -1) for k in range(8)
        ]
        for r in range(4):
            for q in range(4):
                block = jnp.zeros((TILE, TILE), BF)
                for k in range(8):
                    block = lax.select(place[k] == r * 4 + q, tiles[s, k], block)
                a[s, r * TILE : (r + 1) * TILE, q * TILE : (q + 1) * TILE] = block

    loop(5, densify)
    loads[2].wait()

    def own_s(i):
        sacc[span(i, SUB), :] = dot(a[2, span(i, SUB), :], x[...])

    loop(N // SUB, own_s)

    pcopies = []
    for i, o in enumerate(OFFS):

        def product(k, i=i, o=o):
            pbuf[i, span(k, SUB), :] = dot_tn(a[o + 2, :, span(k, SUB)], cot[...]).astype(BF)

        loop(N // SUB, product)
        pcopies.append(sems.copy(pbuf.at[i], pr.at[i], near(o)))

    def own_c(k):
        cacc[span(k, SUB), :] = dot_tn(a[2, :, span(k, SUB)], cot[...])

    loop(N // SUB, own_c)

    scopies = []
    for j in range(XCH):
        cs = pl.ds(j * XW, XW)
        for i, o in enumerate(OFFS):
            xcopies[j][i].wait_recv()

            def add(k, i=i, o=o):
                rs = span(k, SUB)
                total = sacc[rs, cs] + dot(a[o + 2, rs, :], xg[i, :, cs])
                if i == len(OFFS) - 1:
                    sfull[f, rs, cs] = total.astype(BF)
                else:
                    sacc[rs, cs] = total

            loop(N // SUB, add)
        scopies.append(sems.copy(sfull.at[f, :, cs], sfull.at[f, :, cs], peer))

    loads[3].wait()

    def pre_own(k):
        rs = span(k, SUB)
        pre[rs, :] = dot(sfull[f, rs, :], win[f])

    loop(N // SUB, pre_own)
    for j in range(XCH - 1):
        cs = pl.ds(j * XW, XW)
        scopies[j].wait_recv()

        def pre_add(k):
            rs = span(k, SUB)
            pre[rs, :] += dot(sfull[nf, rs, cs], win[nf, cs, :])

        loop(N // SUB, pre_add)
    cs = pl.ds((XCH - 1) * XW, XW)
    scopies[-1].wait_recv()
    hcopies = []
    for j in range(RCH):

        def act(k, j=j):
            rs = pl.ds(pl.multiple_of(j * RW + k * TILE, TILE), TILE)
            v = pre[rs, :] + dot(sfull[nf, rs, cs], win[nf, cs, :])
            g = 1.0 / (1.0 + jnp.exp(-v))
            hfull[f, rs, :] = (v * g).astype(BF)
            dact[rs, :] = g * (1.0 + v * (1.0 - g))

        loop(RW // TILE, act)
        rs = pl.ds(j * RW, RW)
        hcopies.append(sems.copy(hfull.at[f, rs, :], hfull.at[f, rs, :], peer))

    loads[4].wait()

    def z_own(k):
        rs = span(k, SUB)
        zacc[rs, :] = dot(hfull[f, rs, :], wout[f])

    loop(N // SUB, z_own)
    zcopies = []
    for j in range(RCH):
        hcopies[j].wait_recv()
        rs = pl.ds(j * RW, RW)
        z[rs, :] = (zacc[rs, :] + dot(hfull[nf, rs, :], wout[nf])).astype(BF)
        zcopies.append(
            [sems.copy(z.at[rs, :], zg.at[i, rs, :], near(-o)) for i, o in enumerate(OFFS)]
        )

    for i in range(len(OFFS)):
        pcopies[i].wait_recv()

    def close_c(k):
        rs = span(k, TILE)
        total = cacc[rs, :]
        for i in range(len(OFFS)):
            total += pr[i, rs, :].astype(F32)
        cp[rs, :] = total.astype(BF)

    loop(N // TILE, close_c)

    def bh_other(k):
        rs = span(k, SUB)
        bhs[rs, :] = dot_nt(cp[rs, :], wout[nf]).astype(BF)

    loop(N // SUB, bh_other)
    bhcopy = sems.copy(bhs, bhr, peer)

    def gout_rows(k):
        part = dot_tn(hfull[k // 4, :, span(lax.rem(k, 4), TILE)], cp[...])
        g2[k] = part.reshape(NY, NX, NC, 8, W)

    loop(NZ, gout_rows)
    g2core = sems.copy(g2.at[:, :, :, nc], g2c, partner)

    def bh_own(k):
        rs = span(k, SUB)
        cacc[rs, :] = dot_nt(cp[rs, :], wout[f])

    loop(N // SUB, bh_own)

    g2core.wait_recv()

    def g2_first(k):
        g2r1[k] = fold(g2[k, :, :, c] + g2c[k]).astype(BF)

    loop(NZ, g2_first)
    g2zc = [
        sems.copy(g2r1.at[zz], g2z.at[d], node(zz, iy, ix, c)) for d, zz in enumerate(zpeers)
    ]

    bhcopy.wait_recv()

    def close_bp(k):
        rs = span(k, TILE)
        bp[rs, :] = ((cacc[rs, :] + bhr[rs, :].astype(F32)) * dact[rs, :]).astype(BF)

    loop(N // TILE, close_bp)

    def gin_rows(k):
        part = dot_tn(sfull[k // 4, :, span(lax.rem(k, 4), TILE)], bp[...])
        g1[k] = part.reshape(NY, NX, NC, 8, W)

    loop(NZ, gin_rows)
    g1core = sems.copy(g1.at[:, :, :, nc], g1c, partner)

    def own_o(k):
        rs = span(k, SUB)
        oacc[rs, :] = dot(a[2, rs, :], z[...])

    loop(N // SUB, own_o)

    g1core.wait_recv()

    def g1_first(k):
        g1r1[k] = fold(g1[k, :, :, c] + g1c[k]).astype(BF)

    loop(NZ, g1_first)
    g1xc = [
        sems.copy(g1r1.at[:, :, xx], g1x.at[d], node(iz, iy, xx, c))
        for d, xx in enumerate(xpeers)
    ]

    for j in range(RCH):
        ks = pl.ds(j * RW, RW)
        for i, o in enumerate(OFFS):
            zcopies[j][i].wait_recv()

            def out_add(k, i=i, o=o):
                rs = span(k, SUB)
                total = oacc[rs, :] + dot(a[o + 2, rs, ks], zg[i, ks, :])
                if i == len(OFFS) - 1 and j == RCH - 1:
                    out_o[rs, :] = total.astype(BF)
                else:
                    oacc[rs, :] = total

            loop(N // SUB, out_add)

    for copy in g2zc:
        copy.wait_recv()
    total = fold(g2[iz, :, :, c] + g2c[iz])
    for d in range(NZ - 1):
        total += g2z[d].astype(F32)
    g2r2f[...] = total
    g2r2[...] = total.astype(BF)
    g2xc = [
        sems.copy(g2r2.at[:, xx], g2x.at[d], node(iz, iy, xx, c)) for d, xx in enumerate(xpeers)
    ]

    for copy in g1xc:
        copy.wait_recv()

    def g1_second(k):
        total = fold(g1[k, :, ix, c] + g1c[k, :, ix])
        for d in range(NX - 1):
            total += g1x[d, k].astype(F32)
        g1r2f[k] = total
        g1r2[k] = total.astype(BF)

    loop(NZ, g1_second)
    g1yc = sems.copy(g1r2.at[:, ypeer], g1y, node(iz, ypeer, ix, c))

    for copy in g2xc:
        copy.wait_recv()
    total = g2r2f[:, ix]
    for d in range(NX - 1):
        total += g2x[d].astype(F32)
    g2r3f[...] = total
    g2r3[...] = total.astype(BF)
    g2yc = sems.copy(g2r3.at[ypeer], g2y, node(iz, ypeer, ix, c))

    g1yc.wait_recv()
    total = g1r2f[:, iy] + g1y[...].astype(F32)
    g1r3f[...] = total
    g1r3[...] = total.astype(BF)
    g1zc = [
        sems.copy(g1r3.at[zz], g1z.at[d], node(zz, iy, ix, c)) for d, zz in enumerate(zpeers)
    ]

    g2yc.wait_recv()
    total = g2r3f[iy] + g2y[...].astype(F32)
    gout_o[:, : W // 2] = total[:8]
    gout_o[:, W // 2 :] = total[8:]

    for copy in g1zc:
        copy.wait_recv()
    total = g1r3f[iz]
    for d in range(NZ - 1):
        total += g1z[d].astype(F32)
    gin_o[:, : W // 2] = total[:8]
    gin_o[:, W // 2 :] = total[8:]

    sent = [copy for group in xcopies + zcopies for copy in group] + pcopies + scopies + hcopies
    sent += [bhcopy, g2core, g1core, g1yc, g2yc] + g2zc + g1xc + g2xc + g1zc
    for copy in sent:
        copy.wait_send()


def shards(features, weight_in, weight_out, adj_tiles, tile_rows, tile_cols, tile_counts, cotangent):
    anyspace = pl.BlockSpec(memory_space=pl.ANY)
    smem = pl.BlockSpec(memory_space=pltpu.SMEM)
    vmem = pl.BlockSpec(memory_space=pltpu.VMEM)
    V = pltpu.VMEM
    scratch = [
        V((N, W), BF), V((2, 512, W), BF), V((2, 512, W), BF), V((5, 8, TILE, TILE), BF), V((N, W), BF),
        V((5, N, N), BF), V((4, N, W), BF), V((N, W), F32), V((2, N, W), BF), V((N, W), F32),
        V((2, N, W), BF), V((N, W), F32), V((N, W), F32), V((N, W), BF), V((4, N, W), BF),
        V((4, N, W), BF), V((4, N, W), BF), V((N, W), F32), V((N, W), BF), V((N, W), BF),
        V((N, W), BF), V((N, W), BF), V((N, W), F32),
        V((NZ, NY, NX, NC, 8, W), F32), V((NZ, NY, NX, 8, W), F32), V((NZ, NY, NX, 16, W // 2), BF),
        V((3, NZ, NY, 16, W // 2), BF), V((NZ, NY, 16, W // 2), F32), V((NZ, NY, 16, W // 2), BF),
        V((NZ, 16, W // 2), BF), V((NZ, 16, W // 2), F32), V((NZ, 16, W // 2), BF),
        V((7, 16, W // 2), BF),
        V((NZ, NY, NX, NC, 8, W), F32), V((NZ, NY, NX, 8, W), F32), V((NZ, NY, NX, 16, W // 2), BF),
        V((7, NY, NX, 16, W // 2), BF), V((NY, NX, 16, W // 2), F32), V((NY, NX, 16, W // 2), BF),
        V((3, NY, 16, W // 2), BF), V((NY, 16, W // 2), F32), V((NY, 16, W // 2), BF),
        V((16, W // 2), BF),
        pltpu.SemaphoreType.DMA((5,)),
        pltpu.SemaphoreType.DMA((NREMOTE,)),
        pltpu.SemaphoreType.DMA((NREMOTE,)),
    ]
    return pl.pallas_call(
        kernel,
        out_shape=(
            jax.ShapeDtypeStruct((N, W), BF),
            jax.ShapeDtypeStruct((8, W), F32),
            jax.ShapeDtypeStruct((8, W), F32),
        ),
        in_specs=[anyspace, anyspace, anyspace, anyspace, smem, smem, smem, anyspace],
        out_specs=(vmem, vmem, vmem),
        scratch_shapes=scratch,
        compiler_params=pltpu.CompilerParams(
            collective_id=0, has_side_effects=True, vmem_limit_bytes=60 * 1024 * 1024
        ),
        name="graph_layers",
    )(
        features,
        weight_in.reshape(2, 512, W),
        weight_out.reshape(2, 512, W),
        adj_tiles.reshape(5, 8, TILE, TILE),
        tile_rows,
        tile_cols,
        tile_counts,
        cotangent,
    )


def solution(mesh):
    return jax.shard_map(
        shards,
        mesh=mesh,
        in_specs=(
            P("blk", "feat"),
            P(None, "feat"),
            P(None, "feat"),
            P("blk", None, None, None, None),
            P("blk", None, None),
            P("blk", None, None),
            P("blk", None),
            P("blk", "feat"),
        ),
        out_specs=(P("blk", "feat"), P("blk", "feat"), P("blk", "feat")),
        check_vma=False,
    )
```

```python
import functools

import jax
import jax.numpy as jnp
from jax import lax
from jax.experimental import pallas as pl
from jax.experimental.pallas import tpu as pltpu
from jax.sharding import PartitionSpec as P

F32 = jnp.float32
BF = jnp.bfloat16
MESH = pl.DeviceIdType.MESH
NB = 128
NZ, NY, NX, NC = 8, 2, 4, 2
N = 512
W = 512
TILE = 128
XCH = 2
XW = W // XCH
RCH = 2
PWHEN = 0
RW = N // RCH
SUB = 256


def dot(a, b):
    return jnp.dot(a, b, preferred_element_type=F32)


def dot_tn(a, b):
    return lax.dot_general(a, b, (((0,), (0,)), ((), ())), preferred_element_type=F32)


def dot_nt(a, b):
    return lax.dot_general(a, b, (((1,), (1,)), ((), ())), preferred_element_type=F32)


def fold(v):
    return jnp.concatenate([v[..., : W // 2], v[..., W // 2 :]], axis=-2)


def loop(count, body):
    def step(i, carry):
        body(i)
        return carry

    lax.fori_loop(0, count, step, 0)


def span(i, size):
    return pl.ds(pl.multiple_of(i * size, size), size)


class Sems:
    def __init__(self, send, recv):
        self.send, self.recv, self.used = send, recv, 0

    def copy(self, src, dst, device):
        i = self.used
        self.used += 1
        made = pltpu.make_async_remote_copy(
            src_ref=src,
            dst_ref=dst,
            send_sem=self.send.at[i],
            recv_sem=self.recv.at[i],
            device_id=device,
            device_id_type=MESH,
        )
        made.start()
        return made


NREMOTE = 80


def kernel(
    x_h, win_h, wout_h, tiles_h, rows, cols, cnts, cot_h,
    out_o, gin_o, gout_o,
    x, win, wout, tiles, cot,
    a, xg, sacc, sfull, pre, hfull, dact, zacc, z, zg,
    pbuf, pr, cacc, cp, bhs, bhr, bp, oacc,
    g1, g1c, g1r1, g1x, g1r2f, g1r2, g1y, g1r3f, g1r3, g1z,
    g2, g2c, g2r1, g2z, g2r2f, g2r2, g2x, g2r3f, g2r3, g2y,
    lsem, ssem, rsem,
):
    b = lax.axis_index("blk")
    f = lax.axis_index("feat")
    c = lax.rem(b, NC)
    ix = lax.rem(b // NC, NX)
    iy = lax.rem(b // (NC * NX), NY)
    iz = b // (NC * NX * NY)
    nf = 1 - f
    nc = 1 - c

    def node(zz, yy, xx, cc):
        return (((zz * NY + yy) * NX + xx) * NC + cc, f)

    def near(o):
        return (lax.rem(b + o + NB, NB), f)

    peer = (b, nf)
    partner = node(iz, iy, ix, nc)
    xpeers = [lax.rem(ix + d, NX) for d in range(1, NX)]
    zpeers = [lax.rem(iz + d, NZ) for d in range(1, NZ)]
    ypeer = 1 - iy

    greeted = [near(2), near(-2), peer, partner]
    greeted += [node(iz, iy, xx, c) for xx in xpeers]
    greeted += [node(zz, iy, ix, c) for zz in zpeers]
    greeted += [node(iz, ypeer, ix, c)]
    barrier = pltpu.get_barrier_semaphore()
    for device in greeted:
        pl.semaphore_signal(barrier, inc=1, device_id=device, device_id_type=MESH)
    loads = []
    for i, (src, dst) in enumerate(
        ((x_h, x), (tiles_h, tiles), (cot_h, cot), (win_h, win), (wout_h, wout))
    ):
        made = pltpu.make_async_copy(src, dst, lsem.at[i])
        made.start()
        loads.append(made)
    loads[0].wait()
    pl.semaphore_wait(barrier, len(greeted))

    sems = Sems(ssem, rsem)
    step_of = (0, 4, 3 - 2 * c, 1 + 2 * c)

    def spread(src, dst):
        return [
            sems.copy(src, dst(0), near(2)),
            sems.copy(src, dst(1), near(-2)),
            sems.copy(src, dst(2), partner),
        ]

    def on_side(copies, side):
        @pl.when(side == 0)
        def _():
            copies[0].wait_recv()

        @pl.when(side == 1)
        def _():
            copies[1].wait_recv()

    xcopies = []
    for j in range(XCH):
        cs = pl.ds(j * XW, XW)
        xcopies.append(spread(x.at[:, cs], lambda i, cs=cs: xg.at[i, :, cs]))

    loads[1].wait()

    def densify(s):
        live = cnts[0, s]
        place = [
            jnp.where(k < live, rows[s, 0, k] * 4 + cols[s, 0, k], -1) for k in range(8)
        ]
        for r in range(4):
            for q in range(4):
                block = jnp.zeros((TILE, TILE), BF)
                for k in range(8):
                    block = lax.select(place[k] == r * 4 + q, tiles[s, k], block)
                a[s, r * TILE : (r + 1) * TILE, q * TILE : (q + 1) * TILE] = block

    loop(5, densify)
    loads[2].wait()

    def own_s(i):
        sacc[span(i, SUB), :] = dot(a[2, span(i, SUB), :], x[...])

    loop(N // SUB, own_s)


    def product(slot, step, helped):
        def rows_of(k):
            rs = span(k, SUB)
            part = dot_tn(a[step, :, rs], cot[...])
            if helped:
                part += pr[3, rs, :].astype(F32)
            pbuf[slot, rs, :] = part.astype(BF)

        loop(N // SUB, rows_of)

    product(2, step_of[2], False)
    pcopies = [sems.copy(pbuf.at[2], pr.at[2], partner)]
    product(3, step_of[3], False)
    help_copy = sems.copy(pbuf.at[3], pr.at[3], partner)
    product(c, 4 * c, False)

    def own_c(k):
        cacc[span(k, SUB), :] = dot_tn(a[2, :, span(k, SUB)], cot[...])

    loop(N // SUB, own_c)
    help_copy.wait_recv()
    product(nc, 4 * nc, True)

    def send_products():
        pcopies.append(sems.copy(pbuf.at[c], pr.at[c], near(4 * c - 2)))
        pcopies.append(sems.copy(pbuf.at[nc], pr.at[nc], near(4 * nc - 2)))

    if PWHEN == 0:
        send_products()
    scopies = []
    relays = []
    for j in range(XCH):
        cs = pl.ds(j * XW, XW)

        def add(i, last=False):
            def rows_of(k):
                rs = span(k, SUB)
                total = sacc[rs, cs] + dot(a[step_of[i], rs, :], xg[i, :, cs])
                if last:
                    sfull[f, rs, cs] = total.astype(BF)
                else:
                    sacc[rs, cs] = total

            loop(N // SUB, rows_of)

        xcopies[j][2].wait_recv()
        add(2)
        on_side(xcopies[j], nc)
        relay = sems.copy(xg.at[nc, :, cs], xg.at[3, :, cs], partner)
        relays.append(relay)
        on_side(xcopies[j], c)
        add(0)
        add(1)
        relay.wait_recv()
        add(3, True)
        scopies.append(sems.copy(sfull.at[f, :, cs], sfull.at[f, :, cs], peer))
    if PWHEN == 1:
        send_products()

    loads[3].wait()

    def pre_own(k):
        rs = span(k, SUB)
        pre[rs, :] = dot(sfull[f, rs, :], win[f])

    loop(N // SUB, pre_own)
    for j in range(XCH - 1):
        cs = pl.ds(j * XW, XW)
        scopies[j].wait_recv()

        def pre_add(k):
            rs = span(k, SUB)
            pre[rs, :] += dot(sfull[nf, rs, cs], win[nf, cs, :])

        loop(N // SUB, pre_add)
    cs = pl.ds((XCH - 1) * XW, XW)
    scopies[-1].wait_recv()
    if PWHEN == 2:
        send_products()
    hcopies = []
    for j in range(RCH):

        def act(k, j=j):
            rs = pl.ds(pl.multiple_of(j * RW + k * TILE, TILE), TILE)
            v = pre[rs, :] + dot(sfull[nf, rs, cs], win[nf, cs, :])
            g = 1.0 / (1.0 + jnp.exp(-v))
            hfull[f, rs, :] = (v * g).astype(BF)
            dact[rs, :] = g * (1.0 + v * (1.0 - g))

        loop(RW // TILE, act)
        rs = pl.ds(j * RW, RW)
        hcopies.append(sems.copy(hfull.at[f, rs, :], hfull.at[f, rs, :], peer))

    loads[4].wait()

    def z_own(k):
        rs = span(k, SUB)
        zacc[rs, :] = dot(hfull[f, rs, :], wout[f])

    loop(N // SUB, z_own)
    zcopies = []
    for j in range(RCH):
        hcopies[j].wait_recv()
        rs = pl.ds(j * RW, RW)
        z[rs, :] = (zacc[rs, :] + dot(hfull[nf, rs, :], wout[nf])).astype(BF)
        zcopies.append(spread(z.at[rs, :], lambda i, rs=rs: zg.at[i, rs, :]))

    for copy in pcopies:
        copy.wait_recv()

    def close_c(k):
        rs = span(k, TILE)
        total = cacc[rs, :]
        for i in range(3):
            total += pr[i, rs, :].astype(F32)
        cp[rs, :] = total.astype(BF)

    loop(N // TILE, close_c)

    def bh_other(k):
        rs = span(k, SUB)
        bhs[rs, :] = dot_nt(cp[rs, :], wout[nf]).astype(BF)

    loop(N // SUB, bh_other)
    bhcopy = sems.copy(bhs, bhr, peer)

    def gout_rows(k):
        part = dot_tn(hfull[k // 4, :, span(lax.rem(k, 4), TILE)], cp[...])
        g2[k] = part.reshape(NY, NX, NC, 8, W)

    loop(NZ, gout_rows)
    g2core = sems.copy(g2.at[:, :, :, nc], g2c, partner)

    def bh_own(k):
        rs = span(k, SUB)
        cacc[rs, :] = dot_nt(cp[rs, :], wout[f])

    loop(N // SUB, bh_own)

    g2core.wait_recv()

    def g2_first(k):
        g2r1[k] = fold(g2[k, :, :, c] + g2c[k]).astype(BF)

    loop(NZ, g2_first)
    g2zc = [
        sems.copy(g2r1.at[zz], g2z.at[d], node(zz, iy, ix, c)) for d, zz in enumerate(zpeers)
    ]

    bhcopy.wait_recv()

    def close_bp(k):
        rs = span(k, TILE)
        bp[rs, :] = ((cacc[rs, :] + bhr[rs, :].astype(F32)) * dact[rs, :]).astype(BF)

    loop(N // TILE, close_bp)

    def gin_rows(k):
        part = dot_tn(sfull[k // 4, :, span(lax.rem(k, 4), TILE)], bp[...])
        g1[k] = part.reshape(NY, NX, NC, 8, W)

    loop(NZ, gin_rows)
    g1core = sems.copy(g1.at[:, :, :, nc], g1c, partner)

    def own_o(k):
        rs = span(k, SUB)
        oacc[rs, :] = dot(a[2, rs, :], z[...])

    loop(N // SUB, own_o)

    g1core.wait_recv()

    def g1_first(k):
        g1r1[k] = fold(g1[k, :, :, c] + g1c[k]).astype(BF)

    loop(NZ, g1_first)
    g1xc = [
        sems.copy(g1r1.at[:, :, xx], g1x.at[d], node(iz, iy, xx, c))
        for d, xx in enumerate(xpeers)
    ]

    for j in range(RCH):
        ks = pl.ds(j * RW, RW)
        on_side(zcopies[j], nc)
        relays.append(sems.copy(zg.at[nc, ks, :], zg.at[3, ks, :], partner))
        zcopies[j][2].wait_recv()
        on_side(zcopies[j], c)

    def out_add(k):
        rs = span(k, SUB)
        total = oacc[rs, :]
        for i in range(3):
            total += dot(a[step_of[i], rs, :], zg[i])
        oacc[rs, :] = total

    loop(N // SUB, out_add)
    for relay in relays[XCH:]:
        relay.wait_recv()

    def out_last(k):
        rs = span(k, SUB)
        out_o[rs, :] = (oacc[rs, :] + dot(a[step_of[3], rs, :], zg[3])).astype(BF)

    loop(N // SUB, out_last)

    for copy in g2zc:
        copy.wait_recv()
    total = fold(g2[iz, :, :, c] + g2c[iz])
    for d in range(NZ - 1):
        total += g2z[d].astype(F32)
    g2r2f[...] = total
    g2r2[...] = total.astype(BF)
    g2xc = [
        sems.copy(g2r2.at[:, xx], g2x.at[d], node(iz, iy, xx, c)) for d, xx in enumerate(xpeers)
    ]

    for copy in g1xc:
        copy.wait_recv()

    def g1_second(k):
        total = fold(g1[k, :, ix, c] + g1c[k, :, ix])
        for d in range(NX - 1):
            total += g1x[d, k].astype(F32)
        g1r2f[k] = total
        g1r2[k] = total.astype(BF)

    loop(NZ, g1_second)
    g1yc = sems.copy(g1r2.at[:, ypeer], g1y, node(iz, ypeer, ix, c))

    for copy in g2xc:
        copy.wait_recv()
    total = g2r2f[:, ix]
    for d in range(NX - 1):
        total += g2x[d].astype(F32)
    g2r3f[...] = total
    g2r3[...] = total.astype(BF)
    g2yc = sems.copy(g2r3.at[ypeer], g2y, node(iz, ypeer, ix, c))

    g1yc.wait_recv()
    total = g1r2f[:, iy] + g1y[...].astype(F32)
    g1r3f[...] = total
    g1r3[...] = total.astype(BF)
    g1zc = [
        sems.copy(g1r3.at[zz], g1z.at[d], node(zz, iy, ix, c)) for d, zz in enumerate(zpeers)
    ]

    g2yc.wait_recv()
    total = g2r3f[iy] + g2y[...].astype(F32)
    gout_o[:, : W // 2] = total[:8]
    gout_o[:, W // 2 :] = total[8:]

    for copy in g1zc:
        copy.wait_recv()
    total = g1r3f[iz]
    for d in range(NZ - 1):
        total += g1z[d].astype(F32)
    gin_o[:, : W // 2] = total[:8]
    gin_o[:, W // 2 :] = total[8:]

    sent = [copy for group in xcopies + zcopies for copy in group] + pcopies + scopies + hcopies + relays
    sent += [help_copy, bhcopy, g2core, g1core, g1yc, g2yc] + g2zc + g1xc + g2xc + g1zc
    for copy in sent:
        copy.wait_send()


def hand_over(a_ref, b_ref, c_ref, a_o, b_o, c_o):
    a_o[...] = a_ref[...]
    b_o[...] = b_ref[...]
    c_o[...] = c_ref[...]


def shards(features, weight_in, weight_out, adj_tiles, tile_rows, tile_cols, tile_counts, cotangent):
    anyspace = pl.BlockSpec(memory_space=pl.ANY)
    smem = pl.BlockSpec(memory_space=pltpu.SMEM)
    vmem = pl.BlockSpec(memory_space=pltpu.VMEM)
    V = pltpu.VMEM
    scratch = [
        V((N, W), BF), V((2, 512, W), BF), V((2, 512, W), BF), V((5, 8, TILE, TILE), BF), V((N, W), BF),
        V((5, N, N), BF), V((4, N, W), BF), V((N, W), F32), V((2, N, W), BF), V((N, W), F32),
        V((2, N, W), BF), V((N, W), F32), V((N, W), F32), V((N, W), BF), V((4, N, W), BF),
        V((4, N, W), BF), V((4, N, W), BF), V((N, W), F32), V((N, W), BF), V((N, W), BF),
        V((N, W), BF), V((N, W), BF), V((N, W), F32),
        V((NZ, NY, NX, NC, 8, W), F32), V((NZ, NY, NX, 8, W), F32), V((NZ, NY, NX, 16, W // 2), BF),
        V((3, NZ, NY, 16, W // 2), BF), V((NZ, NY, 16, W // 2), F32), V((NZ, NY, 16, W // 2), BF),
        V((NZ, 16, W // 2), BF), V((NZ, 16, W // 2), F32), V((NZ, 16, W // 2), BF),
        V((7, 16, W // 2), BF),
        V((NZ, NY, NX, NC, 8, W), F32), V((NZ, NY, NX, 8, W), F32), V((NZ, NY, NX, 16, W // 2), BF),
        V((7, NY, NX, 16, W // 2), BF), V((NY, NX, 16, W // 2), F32), V((NY, NX, 16, W // 2), BF),
        V((3, NY, 16, W // 2), BF), V((NY, 16, W // 2), F32), V((NY, 16, W // 2), BF),
        V((16, W // 2), BF),
        pltpu.SemaphoreType.DMA((5,)),
        pltpu.SemaphoreType.DMA((NREMOTE,)),
        pltpu.SemaphoreType.DMA((NREMOTE,)),
    ]
    results = pl.pallas_call(
        kernel,
        out_shape=(
            jax.ShapeDtypeStruct((N, W), BF),
            jax.ShapeDtypeStruct((8, W), F32),
            jax.ShapeDtypeStruct((8, W), F32),
        ),
        in_specs=[anyspace, anyspace, anyspace, anyspace, smem, smem, smem, anyspace],
        out_specs=(vmem, vmem, vmem),
        scratch_shapes=scratch,
        compiler_params=pltpu.CompilerParams(
            collective_id=0, has_side_effects=True, vmem_limit_bytes=60 * 1024 * 1024
        ),
        name="graph_layers",
    )(
        features,
        weight_in.reshape(2, 512, W),
        weight_out.reshape(2, 512, W),
        adj_tiles.reshape(5, 8, TILE, TILE),
        tile_rows.transpose(1, 0, 2),
        tile_cols.transpose(1, 0, 2),
        tile_counts,
        cotangent,
    )
    return pl.pallas_call(
        hand_over,
        out_shape=tuple(jax.ShapeDtypeStruct(r.shape, r.dtype) for r in results),
        in_specs=[vmem] * 3,
        out_specs=[vmem] * 3,
        name="hand_over",
    )(*results)


def solution(mesh):
    return jax.shard_map(
        shards,
        mesh=mesh,
        in_specs=(
            P("blk", "feat"),
            P(None, "feat"),
            P(None, "feat"),
            P("blk", None, None, None, None),
            P("blk", None, None),
            P("blk", None, None),
            P("blk", None),
            P("blk", "feat"),
        ),
        out_specs=(P("blk", "feat"), P("blk", "feat"), P("blk", "feat")),
        check_vma=False,
    )
```

```python
import functools

import jax
import jax.numpy as jnp
from jax import lax
from jax.experimental import pallas as pl
from jax.experimental.pallas import tpu as pltpu
from jax.sharding import PartitionSpec as P

F32 = jnp.float32
BF = jnp.bfloat16
MESH = pl.DeviceIdType.MESH
NB = 128
NZ, NY, NX, NC = 8, 2, 4, 2
N = 512
W = 512
TILE = 128
XCH = 2
XW = W // XCH
RCH = 2
PWHEN = 0
RW = N // RCH
SUB = 256


def dot(a, b):
    return jnp.dot(a, b, preferred_element_type=F32)


def dot_tn(a, b):
    return lax.dot_general(a, b, (((0,), (0,)), ((), ())), preferred_element_type=F32)


def dot_nt(a, b):
    return lax.dot_general(a, b, (((1,), (1,)), ((), ())), preferred_element_type=F32)


def fold(v):
    return jnp.concatenate([v[..., : W // 2], v[..., W // 2 :]], axis=-2)


def loop(count, body):
    def step(i, carry):
        body(i)
        return carry

    lax.fori_loop(0, count, step, 0)


def span(i, size):
    return pl.ds(pl.multiple_of(i * size, size), size)


class Sems:
    def __init__(self, send, recv):
        self.send, self.recv, self.used = send, recv, 0

    def make(self, src, dst, device):
        i = self.used
        self.used += 1
        return pltpu.make_async_remote_copy(
            src_ref=src,
            dst_ref=dst,
            send_sem=self.send.at[i],
            recv_sem=self.recv.at[i],
            device_id=device,
            device_id_type=MESH,
        )

    def copy(self, src, dst, device):
        made = self.make(src, dst, device)
        made.start()
        return made


class Swap:
    def __init__(self, sems, edge, lo, hi, way, peer, turn, onward):
        self.edge = edge
        self.lo = sems.copy(lo[0], lo[1], peer)
        self.straight = sems.make(hi[0], hi[1], peer)
        self.out = sems.make(hi[0], way, turn)
        self.on = sems.make(way, hi[2], onward)
        self.pick(self.out.start, self.straight.start)

    def pick(self, at_edge, inside):
        pl.when(self.edge)(lambda: at_edge())
        pl.when(jnp.logical_not(self.edge))(lambda: inside())

    def pass_on(self):
        @pl.when(jnp.logical_not(self.edge))
        def _():
            self.out.wait_recv()
            self.on.start()

    def wait_recv(self):
        self.pass_on()
        self.lo.wait_recv()
        self.pick(self.on.wait_recv, self.straight.wait_recv)

    def wait_send(self):
        self.lo.wait_send()

        def inside():
            self.straight.wait_send()
            self.on.wait_send()

        self.pick(self.out.wait_send, inside)


NREMOTE = 80


def kernel(
    x_h, win_h, wout_h, tiles_h, rows, cols, cnts, cot_h,
    out_o, gin_o, gout_o,
    x, win, wout, tiles, cot,
    a, xg, sacc, sfull, pre, hfull, dact, zacc, z, zg,
    pbuf, pr, cacc, cfull, wq, bp, oacc, sway,
    g1, g1c, g1r1, g1x, g1r2f, g1r2, g1y, g1r3, g1z,
    g2, g2c, g2r1, g2z, g2r2f, g2r2, g2x, g2r3f, g2r3, g2y,
    lsem, ssem, rsem,
):
    b = lax.axis_index("blk")
    f = lax.axis_index("feat")
    c = lax.rem(b, NC)
    ix = lax.rem(b // NC, NX)
    iy = lax.rem(b // (NC * NX), NY)
    iz = b // (NC * NX * NY)
    nf = 1 - f
    nc = 1 - c

    def node(zz, yy, xx, cc):
        return (((zz * NY + yy) * NX + xx) * NC + cc, f)

    def near(o):
        return (lax.rem(b + o + NB, NB), f)

    peer = (b, nf)
    edge = jnp.logical_or(ix == 0, ix == NX - 1)
    beside = ix + 1 - 2 * lax.rem(ix, 2)
    beside_node = (((iz * NY + iy) * NX + beside) * NC + c)
    turn, onward = (beside_node, nf), (beside_node, f)
    partner = node(iz, iy, ix, nc)
    xpeers = [lax.rem(ix + d, NX) for d in range(1, NX)]
    zpeers = [lax.rem(iz + d, NZ) for d in range(1, NZ)]
    ypeer = 1 - iy

    greeted = [near(2), near(-2), peer, partner, turn]
    greeted += [node(iz, iy, xx, c) for xx in xpeers]
    greeted += [node(zz, iy, ix, c) for zz in zpeers]
    greeted += [node(iz, ypeer, ix, c)]

    def owner(zz):
        return (((f * 4 + lax.rem(zz, 4)) * NY + iy) * NX + ix) * NC + c, zz // 4

    def giver(zz):
        return ((zz * NY + iy) * NX + ix) * NC + c, iz // 4

    at_home = iz // 4 == f
    mine = f * 4 + lax.rem(iz, 4)
    greeted += [owner(zz) for zz in zpeers]
    greeted += [giver(lax.rem(mine + d, NZ)) for d in range(1, NZ)]
    barrier = pltpu.get_barrier_semaphore()
    for device in greeted:
        pl.semaphore_signal(barrier, inc=1, device_id=device, device_id_type=MESH)

    @pl.when(jnp.logical_not(at_home))
    def _():
        pl.semaphore_signal(barrier, inc=1, device_id=owner(iz), device_id_type=MESH)
        pl.semaphore_signal(barrier, inc=1, device_id=giver(mine), device_id_type=MESH)

    loads = []
    for i, (src, dst) in enumerate(
        ((x_h, x), (tiles_h, tiles), (cot_h, cot), (win_h, win), (wout_h, wout))
    ):
        made = pltpu.make_async_copy(src, dst, lsem.at[i])
        made.start()
        loads.append(made)
    loads[0].wait()
    pl.semaphore_wait(barrier, len(greeted) + 2 * lax.rem(iz // 4 + f, 2))

    sems = Sems(ssem, rsem)
    step_of = (0, 4, 3 - 2 * c, 1 + 2 * c)

    def swap(ref, out_slot, in_slot, start, size, cs, way):
        half = size // 2
        lo, hi = pl.ds(start, half), pl.ds(start + half, half)
        return Swap(
            sems, edge,
            (ref(out_slot, lo, cs), ref(in_slot[0], lo, cs)),
            (ref(out_slot, hi, cs), ref(in_slot[0], hi, cs), ref(in_slot[1], hi, cs)),
            way, peer, turn, onward,
        )

    def spread(src, dst):
        return [
            sems.copy(src, dst(0), near(2)),
            sems.copy(src, dst(1), near(-2)),
            sems.copy(src, dst(2), partner),
        ]

    def on_side(copies, side):
        @pl.when(side == 0)
        def _():
            copies[0].wait_recv()

        @pl.when(side == 1)
        def _():
            copies[1].wait_recv()

    xcopies = []
    for j in range(XCH):
        cs = pl.ds(j * XW, XW)
        xcopies.append(spread(x.at[:, cs], lambda i, cs=cs: xg.at[i, :, cs]))

    loads[1].wait()

    def densify(s):
        live = cnts[0, s]
        place = [
            jnp.where(k < live, rows[s, 0, k] * 4 + cols[s, 0, k], -1) for k in range(8)
        ]
        for r in range(4):
            for q in range(4):
                block = jnp.zeros((TILE, TILE), BF)
                for k in range(8):
                    block = lax.select(place[k] == r * 4 + q, tiles[s, k], block)
                a[s, r * TILE : (r + 1) * TILE, q * TILE : (q + 1) * TILE] = block

    loop(5, densify)
    loads[2].wait()
    loads[4].wait()
    half = pl.ds(pl.multiple_of(c * (N // 2), N // 2), N // 2)
    wqcopy = sems.copy(wout.at[nf, half, :], wq.at[half, :], peer)

    def own_s(i):
        sacc[span(i, SUB), :] = dot(a[2, span(i, SUB), :], x[...])

    loop(N // SUB, own_s)


    def product(slot, step, helped):
        def rows_of(k):
            rs = span(k, SUB)
            part = dot_tn(a[step, :, rs], cot[...])
            if helped:
                part += pr[3, rs, :].astype(F32)
            pbuf[slot, rs, :] = part.astype(BF)

        loop(N // SUB, rows_of)

    product(2, step_of[2], False)
    pcopies = [sems.copy(pbuf.at[2], pr.at[2], partner)]
    product(3, step_of[3], False)
    help_copy = sems.copy(pbuf.at[3], pr.at[3], partner)
    product(c, 4 * c, False)

    def own_c(k):
        cacc[span(k, SUB), :] = dot_tn(a[2, :, span(k, SUB)], cot[...])

    loop(N // SUB, own_c)
    help_copy.wait_recv()
    product(nc, 4 * nc, True)

    def send_products():
        pcopies.append(sems.copy(pbuf.at[c], pr.at[c], near(4 * c - 2)))
        pcopies.append(sems.copy(pbuf.at[nc], pr.at[nc], near(4 * nc - 2)))

    if PWHEN == 0:
        send_products()
    scopies = []
    relays = []
    for j in range(XCH):
        cs = pl.ds(j * XW, XW)

        def add(i, last=False):
            def rows_of(k):
                rs = span(k, SUB)
                total = sacc[rs, cs] + dot(a[step_of[i], rs, :], xg[i, :, cs])
                if last:
                    sfull[f, rs, cs] = total.astype(BF)
                else:
                    sacc[rs, cs] = total

            loop(N // SUB, rows_of)

        xcopies[j][2].wait_recv()
        add(2)
        on_side(xcopies[j], nc)
        relay = sems.copy(xg.at[nc, :, cs], xg.at[3, :, cs], partner)
        relays.append(relay)
        on_side(xcopies[j], c)
        add(0)
        add(1)
        relay.wait_recv()
        add(3, True)
        scopies.append(
            swap(lambda i, r, q: sfull.at[i, r, q], f, (f, nf), 0, N, cs, sway.at[:, cs])
        )
    if PWHEN == 1:
        send_products()

    wqcopy.wait_recv()
    wqpass = sems.copy(wq.at[half, :], wq.at[half, :], partner)
    loads[3].wait()

    def pre_own(k):
        rs = span(k, SUB)
        pre[rs, :] = dot(sfull[f, rs, :], win[f])

    loop(N // SUB, pre_own)
    for j in range(XCH - 1):
        cs = pl.ds(j * XW, XW)
        scopies[j].wait_recv()

        def pre_add(k):
            rs = span(k, SUB)
            pre[rs, :] += dot(sfull[nf, rs, cs], win[nf, cs, :])

        loop(N // SUB, pre_add)
    cs = pl.ds((XCH - 1) * XW, XW)
    scopies[-1].wait_recv()
    if PWHEN == 2:
        send_products()
    for copy in pcopies:
        copy.wait_recv()

    def close_c(k):
        rs = span(k, TILE)
        total = cacc[rs, :]
        for i in range(3):
            total += pr[i, rs, :].astype(F32)
        cfull[f, rs, :] = total.astype(BF)

    loop(N // TILE, close_c)

    ccopy = sems.copy(cfull.at[f], cfull.at[f], peer)

    hcopies = []
    for j in range(RCH):

        def act(k, j=j):
            rs = pl.ds(pl.multiple_of(j * RW + k * TILE, TILE), TILE)
            v = pre[rs, :] + dot(sfull[nf, rs, cs], win[nf, cs, :])
            g = 1.0 / (1.0 + jnp.exp(-v))
            hfull[f, rs, :] = (v * g).astype(BF)
            dact[rs, :] = g * (1.0 + v * (1.0 - g))

        loop(RW // TILE, act)
        rs = pl.ds(j * RW, RW)
        hcopies.append(sems.copy(hfull.at[f, rs, :], hfull.at[f, rs, :], peer))

    def z_own(k):
        rs = span(k, SUB)
        zacc[rs, :] = dot(hfull[f, rs, :], wout[f])

    loop(N // SUB, z_own)
    def bh_own(k):
        rs = span(k, SUB)
        cacc[rs, :] = dot_nt(cfull[f, rs, :], wout[f])

    loop(N // SUB, bh_own)

    def gout_cols(side):
        def rows_of(k):
            part = dot_tn(hfull[f, :, span(k, TILE)], cfull[side])
            g1[side * 4 + k] = part.reshape(NY, NX, NC, 8, W)

        loop(4, rows_of)

    gout_cols(f)
    ccopy.wait_recv()
    wqpass.wait_recv()

    def close_bp(k):
        rs = span(k, TILE)
        back = cacc[rs, :] + dot_nt(cfull[nf, rs, :], wq[...])
        bp[rs, :] = (back * dact[rs, :]).astype(BF)

    loop(N // TILE, close_bp)

    def gin_rows(k):
        part = dot_tn(sfull[k // 4, :, span(lax.rem(k, 4), TILE)], bp[...])
        g2[k] = part.reshape(NY, NX, NC, 8, W)

    loop(NZ, gin_rows)
    g2core = sems.copy(g2.at[:, :, :, nc], g2c, partner)
    gout_cols(nf)
    g1core = sems.copy(g1.at[:, :, :, nc], g1c, partner)

    g2core.wait_recv()

    def g2_first(k):
        g2r1[k] = fold(g2[k, :, :, c] + g2c[k]).astype(BF)

    loop(NZ, g2_first)
    g2zc = [
        sems.copy(g2r1.at[zz], g2z.at[d], node(zz, iy, ix, c)) for d, zz in enumerate(zpeers)
    ]

    g1core.wait_recv()

    def g1_first(k):
        g1r1[k] = fold(g1[k, :, :, c] + g1c[k]).astype(BF)

    loop(NZ, g1_first)
    g1xc = [
        sems.copy(g1r1.at[:, :, xx], g1x.at[d], node(iz, iy, xx, c))
        for d, xx in enumerate(xpeers)
    ]

    zcopies = []
    for j in range(RCH):
        hcopies[j].wait_recv()
        rs = pl.ds(j * RW, RW)
        z[rs, :] = (zacc[rs, :] + dot(hfull[nf, rs, :], wout[nf])).astype(BF)
        zcopies.append(spread(z.at[rs, :], lambda i, rs=rs: zg.at[i, rs, :]))

    def own_o(k):
        rs = span(k, SUB)
        oacc[rs, :] = dot(a[2, rs, :], z[...])

    loop(N // SUB, own_o)

    for copy in g2zc:
        copy.wait_recv()
    total = fold(g2[iz, :, :, c] + g2c[iz])
    for d in range(NZ - 1):
        total += g2z[d].astype(F32)
    g2r2f[...] = total
    g2r2[...] = total.astype(BF)
    g2xc = [
        sems.copy(g2r2.at[:, xx], g2x.at[d], node(iz, iy, xx, c)) for d, xx in enumerate(xpeers)
    ]

    for j in range(RCH):
        ks = pl.ds(j * RW, RW)
        on_side(zcopies[j], nc)
        relays.append(sems.copy(zg.at[nc, ks, :], zg.at[3, ks, :], partner))
        zcopies[j][2].wait_recv()
        on_side(zcopies[j], c)

    for copy in g1xc:
        copy.wait_recv()

    def g1_second(k):
        total = fold(g1[k, :, ix, c] + g1c[k, :, ix])
        for d in range(NX - 1):
            total += g1x[d, k].astype(F32)
        g1r2f[k] = total
        g1r2[k] = total.astype(BF)

    loop(NZ, g1_second)
    g1yc = sems.copy(g1r2.at[:, ypeer], g1y, node(iz, ypeer, ix, c))

    for copy in g2xc:
        copy.wait_recv()
    total = g2r2f[:, ix]
    for d in range(NX - 1):
        total += g2x[d].astype(F32)
    g2r3f[...] = total
    g2r3[...] = total.astype(BF)
    g2yc = sems.copy(g2r3.at[ypeer], g2y, node(iz, ypeer, ix, c))

    def out_add(k):
        rs = span(k, SUB)
        total = oacc[rs, :]
        for i in range(3):
            total += dot(a[step_of[i], rs, :], zg[i])
        oacc[rs, :] = total

    loop(N // SUB, out_add)
    for relay in relays[XCH:]:
        relay.wait_recv()

    def out_last(k):
        rs = span(k, SUB)
        out_o[rs, :] = (oacc[rs, :] + dot(a[step_of[3], rs, :], zg[3])).astype(BF)

    loop(N // SUB, out_last)

    g1yc.wait_recv()
    total = g1r2f[:, iy] + g1y[...].astype(F32)
    g1r3[...] = total.astype(BF)
    g1zc = [
        sems.copy(g1r3.at[zz], g1z.at[d + 1], owner(zz)) for d, zz in enumerate(zpeers)
    ]
    g1last = sems.make(g1r3.at[iz], g1z.at[0], owner(iz))

    @pl.when(at_home)
    def _():
        g1z[0] = g1r3[iz]

    pl.when(jnp.logical_not(at_home))(lambda: g1last.start())

    g2yc.wait_recv()
    total = g2r3f[iy] + g2y[...].astype(F32)
    gin_o[:, : W // 2] = total[:8]
    gin_o[:, W // 2 :] = total[8:]

    for copy in g1zc:
        copy.wait_recv()
    pl.when(jnp.logical_not(at_home))(lambda: g1last.wait_recv())
    total = g1z[0].astype(F32)
    for d in range(1, NZ):
        total += g1z[d].astype(F32)
    gout_o[:, : W // 2] = total[:8]
    gout_o[:, W // 2 :] = total[8:]

    sent = [copy for group in xcopies + zcopies for copy in group] + pcopies + scopies + hcopies + relays
    sent += [help_copy, wqcopy, wqpass, ccopy, g2core, g1core, g1yc, g2yc] + g2zc + g1xc + g2xc + g1zc
    for copy in sent:
        copy.wait_send()
    pl.when(jnp.logical_not(at_home))(lambda: g1last.wait_send())


def hand_over(a_ref, b_ref, c_ref, a_o, b_o, c_o):
    a_o[...] = a_ref[...]
    b_o[...] = b_ref[...]
    c_o[...] = c_ref[...]


def shards(features, weight_in, weight_out, adj_tiles, tile_rows, tile_cols, tile_counts, cotangent):
    anyspace = pl.BlockSpec(memory_space=pl.ANY)
    smem = pl.BlockSpec(memory_space=pltpu.SMEM)
    vmem = pl.BlockSpec(memory_space=pltpu.VMEM)
    V = pltpu.VMEM
    scratch = [
        V((N, W), BF), V((2, 512, W), BF), V((2, 512, W), BF), V((5, 8, TILE, TILE), BF), V((N, W), BF),
        V((5, N, N), BF), V((4, N, W), BF), V((N, W), F32), V((2, N, W), BF), V((N, W), F32),
        V((2, N, W), BF), V((N, W), F32), V((N, W), F32), V((N, W), BF), V((4, N, W), BF),
        V((4, N, W), BF), V((4, N, W), BF), V((N, W), F32), V((2, N, W), BF), V((N, W), BF),
        V((N, W), BF), V((N, W), F32), V((N // 2, W), BF),
        V((NZ, NY, NX, NC, 8, W), F32), V((NZ, NY, NX, 8, W), F32), V((NZ, NY, NX, 16, W // 2), BF),
        V((3, NZ, NY, 16, W // 2), BF), V((NZ, NY, 16, W // 2), F32), V((NZ, NY, 16, W // 2), BF),
        V((NZ, 16, W // 2), BF), V((NZ, 16, W // 2), BF),
        V((NZ, 16, W // 2), BF),
        V((NZ, NY, NX, NC, 8, W), F32), V((NZ, NY, NX, 8, W), F32), V((NZ, NY, NX, 16, W // 2), BF),
        V((7, NY, NX, 16, W // 2), BF), V((NY, NX, 16, W // 2), F32), V((NY, NX, 16, W // 2), BF),
        V((3, NY, 16, W // 2), BF), V((NY, 16, W // 2), F32), V((NY, 16, W // 2), BF),
        V((16, W // 2), BF),
        pltpu.SemaphoreType.DMA((5,)),
        pltpu.SemaphoreType.DMA((NREMOTE,)),
        pltpu.SemaphoreType.DMA((NREMOTE,)),
    ]
    results = pl.pallas_call(
        kernel,
        out_shape=(
            jax.ShapeDtypeStruct((N, W), BF),
            jax.ShapeDtypeStruct((8, W), F32),
            jax.ShapeDtypeStruct((8, W), F32),
        ),
        in_specs=[anyspace, anyspace, anyspace, anyspace, smem, smem, smem, anyspace],
        out_specs=(vmem, vmem, vmem),
        scratch_shapes=scratch,
        compiler_params=pltpu.CompilerParams(
            collective_id=0, has_side_effects=True, vmem_limit_bytes=60 * 1024 * 1024
        ),
        name="graph_layers",
    )(
        features,
        weight_in.reshape(2, 512, W),
        weight_out.reshape(2, 512, W),
        adj_tiles.reshape(5, 8, TILE, TILE),
        tile_rows.transpose(1, 0, 2),
        tile_cols.transpose(1, 0, 2),
        tile_counts,
        cotangent,
    )
    return pl.pallas_call(
        hand_over,
        out_shape=tuple(jax.ShapeDtypeStruct(r.shape, r.dtype) for r in results),
        in_specs=[vmem] * 3,
        out_specs=[vmem] * 3,
        name="hand_over",
    )(*results)


def solution(mesh):
    return jax.shard_map(
        shards,
        mesh=mesh,
        in_specs=(
            P("blk", "feat"),
            P(None, "feat"),
            P(None, "feat"),
            P("blk", None, None, None, None),
            P("blk", None, None),
            P("blk", None, None),
            P("blk", None),
            P("blk", "feat"),
        ),
        out_specs=(P("blk", "feat"), P("blk", "feat"), P("blk", "feat")),
        check_vma=False,
    )
```

```python
import functools

import jax
import jax.numpy as jnp
from jax import lax
from jax.experimental import pallas as pl
from jax.experimental.pallas import tpu as pltpu
from jax.sharding import PartitionSpec as P

F32 = jnp.float32
BF = jnp.bfloat16
MESH = pl.DeviceIdType.MESH
NB = 128
NZ, NY, NX, NC = 8, 2, 4, 2
N = 512
W = 512
TILE = 128
XCH = 2
XW = W // XCH
RCH = 4
PWHEN = 0
SPLIT = 3
RW = N // RCH
SUB = 256


def dot(a, b):
    return jnp.dot(a, b, preferred_element_type=F32)


def dot_tn(a, b):
    return lax.dot_general(a, b, (((0,), (0,)), ((), ())), preferred_element_type=F32)


def dot_nt(a, b):
    return lax.dot_general(a, b, (((1,), (1,)), ((), ())), preferred_element_type=F32)


def fold(v):
    return jnp.concatenate([v[..., : W // 2], v[..., W // 2 :]], axis=-2)


def loop(count, body):
    def step(i, carry):
        body(i)
        return carry

    lax.fori_loop(0, count, step, 0)


def span(i, size):
    return pl.ds(pl.multiple_of(i * size, size), size)


class Sems:
    def __init__(self, send, recv):
        self.send, self.recv, self.used = send, recv, 0

    def make(self, src, dst, device):
        i = self.used
        self.used += 1
        return pltpu.make_async_remote_copy(
            src_ref=src,
            dst_ref=dst,
            send_sem=self.send.at[i],
            recv_sem=self.recv.at[i],
            device_id=device,
            device_id_type=MESH,
        )

    def copy(self, src, dst, device):
        made = self.make(src, dst, device)
        made.start()
        return made


class Swap:
    def __init__(self, sems, edge, lo, hi, way, peer, turn, onward):
        self.edge = edge
        self.lo = sems.copy(lo[0], lo[1], peer)
        self.straight = sems.make(hi[0], hi[1], peer)
        self.out = sems.make(hi[0], way, turn)
        self.on = sems.make(way, hi[2], onward)
        self.pick(self.out.start, self.straight.start)

    def pick(self, at_edge, inside):
        pl.when(self.edge)(lambda: at_edge())
        pl.when(jnp.logical_not(self.edge))(lambda: inside())

    def pass_on(self):
        @pl.when(jnp.logical_not(self.edge))
        def _():
            self.out.wait_recv()
            self.on.start()

    def wait_recv(self):
        self.pass_on()
        self.lo.wait_recv()
        self.pick(self.on.wait_recv, self.straight.wait_recv)

    def wait_send(self):
        self.lo.wait_send()

        def inside():
            self.straight.wait_send()
            self.on.wait_send()

        self.pick(self.out.wait_send, inside)


NREMOTE = 112


def kernel(
    x_h, win_h, wout_h, tiles_h, rows_h, cols_h, cnts_h, cot_h,
    out_h, gin_h, gout_h,
    rows, cols, cnts, out_o, gin_o, gout_o,
    x, win, wout, tiles, cot,
    a, xg, sacc, sfull, pre, hfull, dact, zacc, z, zg,
    pbuf, pr, cacc, cfull, wq, bp, oacc, sway,
    g1, g1c, g1r1, g1x, g1r2f, g1r2, g1y, g1r3, g1z,
    g2, g2c, g2r1, g2z, g2r2f, g2r2, g2x, g2r3f, g2r3, g2y,
    lsem, ssem, rsem,
):
    b = lax.axis_index("blk")
    f = lax.axis_index("feat")
    c = lax.rem(b, NC)
    ix = lax.rem(b // NC, NX)
    iy = lax.rem(b // (NC * NX), NY)
    iz = b // (NC * NX * NY)
    nf = 1 - f
    nc = 1 - c

    def node(zz, yy, xx, cc):
        return (((zz * NY + yy) * NX + xx) * NC + cc, f)

    def near(o):
        return (lax.rem(b + o + NB, NB), f)

    peer = (b, nf)
    edge = jnp.logical_or(ix == 0, ix == NX - 1)
    beside = ix + 1 - 2 * lax.rem(ix, 2)
    beside_node = (((iz * NY + iy) * NX + beside) * NC + c)
    turn, onward = (beside_node, nf), (beside_node, f)
    across = (((iz * NY + 1 - iy) * NX + ix) * NC + c, nf)
    partner = node(iz, iy, ix, nc)
    xpeers = [lax.rem(ix + d, NX) for d in range(1, NX)]
    zpeers = [lax.rem(iz + d, NZ) for d in range(1, NZ)]
    ypeer = 1 - iy

    greeted = [near(2), near(-2), peer, partner, turn, across]
    greeted += [node(iz, iy, xx, c) for xx in xpeers]
    greeted += [node(zz, iy, ix, c) for zz in zpeers]
    greeted += [node(iz, ypeer, ix, c)]

    def owner(zz):
        return (((f * 4 + lax.rem(zz, 4)) * NY + iy) * NX + ix) * NC + c, zz // 4

    def giver(zz):
        return ((zz * NY + iy) * NX + ix) * NC + c, iz // 4

    at_home = iz // 4 == f
    mine = f * 4 + lax.rem(iz, 4)
    greeted += [owner(zz) for zz in zpeers]
    greeted += [giver(lax.rem(mine + d, NZ)) for d in range(1, NZ)]
    barrier = pltpu.get_barrier_semaphore()
    for device in greeted:
        pl.semaphore_signal(barrier, inc=1, device_id=device, device_id_type=MESH)

    @pl.when(jnp.logical_not(at_home))
    def _():
        pl.semaphore_signal(barrier, inc=1, device_id=owner(iz), device_id_type=MESH)
        pl.semaphore_signal(barrier, inc=1, device_id=giver(mine), device_id_type=MESH)

    loads = []
    for i, (src, dst) in enumerate(
        ((x_h, x), (tiles_h, tiles), (cot_h, cot), (win_h, win), (wout_h, wout),
         (rows_h, rows), (cols_h, cols), (cnts_h, cnts))
    ):
        made = pltpu.make_async_copy(src, dst, lsem.at[i])
        made.start()
        loads.append(made)
    loads[0].wait()
    pl.semaphore_wait(barrier, len(greeted) + 2 * lax.rem(iz // 4 + f, 2))

    sems = Sems(ssem, rsem)
    step_of = (0, 4, 3 - 2 * c, 1 + 2 * c)

    def swap(ref, out_slot, in_slot, start, size, cs, way):
        near_rows = size * SPLIT // 4
        lo, hi = pl.ds(start, near_rows), pl.ds(start + near_rows, size - near_rows)
        return Swap(
            sems, edge,
            (ref(out_slot, lo, cs), ref(in_slot[0], lo, cs)),
            (ref(out_slot, hi, cs), ref(in_slot[0], hi, cs), ref(in_slot[1], hi, cs)),
            way, peer, turn, onward,
        )

    def spread(src, dst):
        return [
            sems.copy(src, dst(0), near(2)),
            sems.copy(src, dst(1), near(-2)),
            sems.copy(src, dst(2), partner),
        ]

    def on_side(copies, side):
        @pl.when(side == 0)
        def _():
            copies[0].wait_recv()

        @pl.when(side == 1)
        def _():
            copies[1].wait_recv()

    xcopies = []
    for j in range(XCH):
        cs = pl.ds(j * XW, XW)
        xcopies.append(spread(x.at[:, cs], lambda i, cs=cs: xg.at[i, :, cs]))

    for i in (1, 5, 6, 7):
        loads[i].wait()

    def densify(s):
        live = cnts[0, s]
        place = [
            jnp.where(k < live, rows[s, 0, k] * 4 + cols[s, 0, k], -1) for k in range(8)
        ]
        for r in range(4):
            for q in range(4):
                block = jnp.zeros((TILE, TILE), BF)
                for k in range(8):
                    block = lax.select(place[k] == r * 4 + q, tiles[s, k], block)
                a[s, r * TILE : (r + 1) * TILE, q * TILE : (q + 1) * TILE] = block

    loop(5, densify)
    loads[2].wait()
    loads[4].wait()
    half = pl.ds(pl.multiple_of(c * (N // 2), N // 2), N // 2)
    wqcopy = sems.copy(wout.at[nf, half, :], wq.at[half, :], across)

    def own_s(i):
        sacc[span(i, SUB), :] = dot(a[2, span(i, SUB), :], x[...])

    loop(N // SUB, own_s)


    def product(slot, step, helped):
        def rows_of(k):
            rs = span(k, SUB)
            part = dot_tn(a[step, :, rs], cot[...])
            if helped:
                part += pr[3, rs, :].astype(F32)
            pbuf[slot, rs, :] = part.astype(BF)

        loop(N // SUB, rows_of)

    product(2, step_of[2], False)
    pcopies = [sems.copy(pbuf.at[2], pr.at[2], partner)]
    product(3, step_of[3], False)
    help_copy = sems.copy(pbuf.at[3], pr.at[3], partner)
    product(c, 4 * c, False)

    def own_c(k):
        cacc[span(k, SUB), :] = dot_tn(a[2, :, span(k, SUB)], cot[...])

    loop(N // SUB, own_c)
    help_copy.wait_recv()
    product(nc, 4 * nc, True)

    def send_products():
        pcopies.append(sems.copy(pbuf.at[c], pr.at[c], near(4 * c - 2)))
        pcopies.append(sems.copy(pbuf.at[nc], pr.at[nc], near(4 * nc - 2)))

    if PWHEN == 0:
        send_products()
    scopies = []
    relays = []
    for j in range(XCH):
        cs = pl.ds(j * XW, XW)

        def add(i, last=False):
            def rows_of(k):
                rs = span(k, SUB)
                total = sacc[rs, cs] + dot(a[step_of[i], rs, :], xg[i, :, cs])
                if last:
                    sfull[f, rs, cs] = total.astype(BF)
                else:
                    sacc[rs, cs] = total

            loop(N // SUB, rows_of)

        xcopies[j][2].wait_recv()
        add(2)
        on_side(xcopies[j], nc)
        relay = sems.copy(xg.at[nc, :, cs], xg.at[3, :, cs], partner)
        relays.append(relay)
        on_side(xcopies[j], c)
        add(0)
        add(1)
        relay.wait_recv()
        add(3, True)
        scopies.append(
            swap(lambda i, r, q: sfull.at[i, r, q], f, (f, nf), 0, N, cs, sway.at[:, cs])
        )
    if PWHEN == 1:
        send_products()

    wqcopy.wait_recv()
    wqpass = sems.copy(wq.at[half, :], wq.at[half, :], partner)
    loads[3].wait()

    def pre_own(k):
        rs = span(k, SUB)
        pre[rs, :] = dot(sfull[f, rs, :], win[f])

    loop(N // SUB, pre_own)
    for j in range(XCH - 1):
        cs = pl.ds(j * XW, XW)
        scopies[j].wait_recv()

        def pre_add(k):
            rs = span(k, SUB)
            pre[rs, :] += dot(sfull[nf, rs, cs], win[nf, cs, :])

        loop(N // SUB, pre_add)
    cs = pl.ds((XCH - 1) * XW, XW)
    scopies[-1].wait_recv()
    if PWHEN == 2:
        send_products()
    for copy in pcopies:
        copy.wait_recv()

    def close_c(k):
        rs = span(k, TILE)
        total = cacc[rs, :]
        for i in range(3):
            total += pr[i, rs, :].astype(F32)
        cfull[f, rs, :] = total.astype(BF)

    loop(N // TILE, close_c)

    ccopy = sems.copy(cfull.at[f], cfull.at[f], peer)

    hcopies = []
    for j in range(RCH):

        def act(k, j=j):
            rs = pl.ds(pl.multiple_of(j * RW + k * TILE, TILE), TILE)
            v = pre[rs, :] + dot(sfull[nf, rs, cs], win[nf, cs, :])
            g = 1.0 / (1.0 + jnp.exp(-v))
            hfull[f, rs, :] = (v * g).astype(BF)
            dact[rs, :] = g * (1.0 + v * (1.0 - g))

        loop(RW // TILE, act)
        rs = pl.ds(j * RW, RW)
        hcopies.append(sems.copy(hfull.at[f, rs, :], hfull.at[f, rs, :], peer))

    def z_own(k):
        rs = span(k, SUB)
        zacc[rs, :] = dot(hfull[f, rs, :], wout[f])

    loop(N // SUB, z_own)
    def bh_own(k):
        rs = span(k, SUB)
        cacc[rs, :] = dot_nt(cfull[f, rs, :], wout[f])

    loop(N // SUB, bh_own)

    def gout_cols(side):
        def rows_of(k):
            part = dot_tn(hfull[f, :, span(k, TILE)], cfull[side])
            g1[side * 4 + k] = part.reshape(NY, NX, NC, 8, W)

        loop(4, rows_of)

    gout_cols(f)
    ccopy.wait_recv()
    wqpass.wait_recv()

    def close_bp(k):
        rs = span(k, TILE)
        back = cacc[rs, :] + dot_nt(cfull[nf, rs, :], wq[...])
        bp[rs, :] = (back * dact[rs, :]).astype(BF)

    loop(N // TILE, close_bp)

    def gin_rows(k):
        part = dot_tn(sfull[k // 4, :, span(lax.rem(k, 4), TILE)], bp[...])
        g2[k] = part.reshape(NY, NX, NC, 8, W)

    loop(NZ, gin_rows)
    g2core = sems.copy(g2.at[:, :, :, nc], g2c, partner)
    gout_cols(nf)
    g1core = sems.copy(g1.at[:, :, :, nc], g1c, partner)

    g2core.wait_recv()

    def g2_first(k):
        g2r1[k] = fold(g2[k, :, :, c] + g2c[k]).astype(BF)

    loop(NZ, g2_first)
    g2zc = [
        sems.copy(g2r1.at[zz], g2z.at[d], node(zz, iy, ix, c)) for d, zz in enumerate(zpeers)
    ]

    g1core.wait_recv()

    def g1_first(k):
        g1r1[k] = fold(g1[k, :, :, c] + g1c[k]).astype(BF)

    loop(NZ, g1_first)
    g1xc = [
        sems.copy(g1r1.at[:, :, xx], g1x.at[d], node(iz, iy, xx, c))
        for d, xx in enumerate(xpeers)
    ]

    zcopies = []
    for j in range(RCH):
        hcopies[j].wait_recv()
        rs = pl.ds(j * RW, RW)
        z[rs, :] = (zacc[rs, :] + dot(hfull[nf, rs, :], wout[nf])).astype(BF)
        zcopies.append(spread(z.at[rs, :], lambda i, rs=rs: zg.at[i, rs, :]))

    def own_o(k):
        rs = span(k, SUB)
        oacc[rs, :] = dot(a[2, rs, :], z[...])

    loop(N // SUB, own_o)

    for copy in g1xc:
        copy.wait_recv()

    def g1_second(k):
        total = fold(g1[k, :, ix, c] + g1c[k, :, ix])
        for d in range(NX - 1):
            total += g1x[d, k].astype(F32)
        g1r2f[k] = total
        g1r2[k] = total.astype(BF)

    loop(NZ, g1_second)
    g1yc = sems.copy(g1r2.at[:, ypeer], g1y, node(iz, ypeer, ix, c))

    for copy in g2zc:
        copy.wait_recv()
    total = fold(g2[iz, :, :, c] + g2c[iz])
    for d in range(NZ - 1):
        total += g2z[d].astype(F32)
    g2r2f[...] = total
    g2r2[...] = total.astype(BF)
    g2xc = [
        sems.copy(g2r2.at[:, xx], g2x.at[d], node(iz, iy, xx, c)) for d, xx in enumerate(xpeers)
    ]

    g1yc.wait_recv()
    total = g1r2f[:, iy] + g1y[...].astype(F32)
    g1r3[...] = total.astype(BF)
    g1zc = [
        sems.copy(g1r3.at[zz], g1z.at[d + 1], owner(zz)) for d, zz in enumerate(zpeers)
    ]
    g1last = sems.make(g1r3.at[iz], g1z.at[0], owner(iz))

    @pl.when(at_home)
    def _():
        g1z[0] = g1r3[iz]

    pl.when(jnp.logical_not(at_home))(lambda: g1last.start())

    for copy in g2xc:
        copy.wait_recv()
    total = g2r2f[:, ix]
    for d in range(NX - 1):
        total += g2x[d].astype(F32)
    g2r3f[...] = total
    g2r3[...] = total.astype(BF)
    g2yc = sems.copy(g2r3.at[ypeer], g2y, node(iz, ypeer, ix, c))

    for j in range(RCH):
        ks = pl.ds(j * RW, RW)
        on_side(zcopies[j], nc)
        relays.append(sems.copy(zg.at[nc, ks, :], zg.at[3, ks, :], partner))
        zcopies[j][2].wait_recv()
        on_side(zcopies[j], c)

    def out_add(k):
        rs = span(k, SUB)
        total = oacc[rs, :]
        for i in range(3):
            total += dot(a[step_of[i], rs, :], zg[i])
        oacc[rs, :] = total

    loop(N // SUB, out_add)
    for relay in relays[XCH:]:
        relay.wait_recv()

    stores = []
    for k in range(N // SUB):
        rs = pl.ds(k * SUB, SUB)
        out_o[rs, :] = (oacc[rs, :] + dot(a[step_of[3], rs, :], zg[3])).astype(BF)
        stores.append(pltpu.make_async_copy(out_o.at[rs, :], out_h.at[rs, :], lsem.at[10 + k]))
        stores[-1].start()

    g2yc.wait_recv()
    total = g2r3f[iy] + g2y[...].astype(F32)
    gin_o[:, : W // 2] = total[:8]
    gin_o[:, W // 2 :] = total[8:]
    stores.append(pltpu.make_async_copy(gin_o, gin_h, lsem.at[8]))
    stores[-1].start()

    for copy in g1zc:
        copy.wait_recv()
    pl.when(jnp.logical_not(at_home))(lambda: g1last.wait_recv())
    total = g1z[0].astype(F32)
    for d in range(1, NZ):
        total += g1z[d].astype(F32)
    gout_o[:, : W // 2] = total[:8]
    gout_o[:, W // 2 :] = total[8:]
    stores.append(pltpu.make_async_copy(gout_o, gout_h, lsem.at[9]))
    stores[-1].start()

    sent = [copy for group in xcopies + zcopies for copy in group] + pcopies + scopies + hcopies + relays
    sent += [help_copy, wqcopy, wqpass, ccopy, g2core, g1core, g1yc, g2yc] + g2zc + g1xc + g2xc + g1zc
    for copy in stores:
        copy.wait()
    for copy in sent:
        copy.wait_send()
    pl.when(jnp.logical_not(at_home))(lambda: g1last.wait_send())


def hand_over(a_ref, b_ref, c_ref, a_o, b_o, c_o, a_v, b_v, c_v, insem, outsem):
    moves = [(b_ref, b_v, b_o), (c_ref, c_v, c_o)]
    for k in range(4):
        rs = pl.ds(k * (N // 4), N // 4)
        moves.append((a_ref.at[rs, :], a_v.at[rs, :], a_o.at[rs, :]))
    taken = [pltpu.make_async_copy(m[0], m[1], insem.at[i]) for i, m in enumerate(moves)]
    given = [pltpu.make_async_copy(m[1], m[2], outsem.at[i]) for i, m in enumerate(moves)]
    for copy in taken:
        copy.start()
    for into, out in zip(taken, given):
        into.wait()
        out.start()
    for copy in given:
        copy.wait()


def shards(features, weight_in, weight_out, adj_tiles, tile_rows, tile_cols, tile_counts, cotangent):
    anyspace = pl.BlockSpec(memory_space=pl.ANY)
    V = pltpu.VMEM
    scratch = [
        pltpu.SMEM((5, 1, 8), jnp.int32), pltpu.SMEM((5, 1, 8), jnp.int32), pltpu.SMEM((1, 5), jnp.int32),
        V((N, W), BF), V((8, W), F32), V((8, W), F32),
        V((N, W), BF), V((2, 512, W), BF), V((2, 512, W), BF), V((5, 8, TILE, TILE), BF), V((N, W), BF),
        V((5, N, N), BF), V((4, N, W), BF), V((N, W), F32), V((2, N, W), BF), V((N, W), F32),
        V((2, N, W), BF), V((N, W), F32), V((N, W), F32), V((N, W), BF), V((4, N, W), BF),
        V((4, N, W), BF), V((4, N, W), BF), V((N, W), F32), V((2, N, W), BF), V((N, W), BF),
        V((N, W), BF), V((N, W), F32), V((N - N * SPLIT // 4, W), BF),
        V((NZ, NY, NX, NC, 8, W), F32), V((NZ, NY, NX, 8, W), F32), V((NZ, NY, NX, 16, W // 2), BF),
        V((3, NZ, NY, 16, W // 2), BF), V((NZ, NY, 16, W // 2), F32), V((NZ, NY, 16, W // 2), BF),
        V((NZ, 16, W // 2), BF), V((NZ, 16, W // 2), BF),
        V((NZ, 16, W // 2), BF),
        V((NZ, NY, NX, NC, 8, W), F32), V((NZ, NY, NX, 8, W), F32), V((NZ, NY, NX, 16, W // 2), BF),
        V((7, NY, NX, 16, W // 2), BF), V((NY, NX, 16, W // 2), F32), V((NY, NX, 16, W // 2), BF),
        V((3, NY, 16, W // 2), BF), V((NY, 16, W // 2), F32), V((NY, 16, W // 2), BF),
        V((16, W // 2), BF),
        pltpu.SemaphoreType.DMA((8 + 2 + N // SUB,)),
        pltpu.SemaphoreType.DMA((NREMOTE,)),
        pltpu.SemaphoreType.DMA((NREMOTE,)),
    ]
    results = pl.pallas_call(
        kernel,
        out_shape=(
            jax.ShapeDtypeStruct((N, W), BF),
            jax.ShapeDtypeStruct((8, W), F32),
            jax.ShapeDtypeStruct((8, W), F32),
        ),
        in_specs=[anyspace] * 8,
        out_specs=(anyspace,) * 3,
        scratch_shapes=scratch,
        compiler_params=pltpu.CompilerParams(
            collective_id=0, has_side_effects=True, vmem_limit_bytes=60 * 1024 * 1024
        ),
        name="graph_layers",
    )(
        features,
        weight_in.reshape(2, 512, W),
        weight_out.reshape(2, 512, W),
        adj_tiles.reshape(5, 8, TILE, TILE),
        tile_rows.transpose(1, 0, 2),
        tile_cols.transpose(1, 0, 2),
        tile_counts,
        cotangent,
    )
    return pl.pallas_call(
        hand_over,
        out_shape=tuple(jax.ShapeDtypeStruct(r.shape, r.dtype) for r in results),
        in_specs=[anyspace] * 3,
        out_specs=[anyspace] * 3,
        scratch_shapes=[
            V((N, W), BF), V((8, W), F32), V((8, W), F32),
            pltpu.SemaphoreType.DMA((6,)), pltpu.SemaphoreType.DMA((6,)),
        ],
        name="hand_over",
    )(*results)


def solution(mesh):
    return jax.shard_map(
        shards,
        mesh=mesh,
        in_specs=(
            P("blk", "feat"),
            P(None, "feat"),
            P(None, "feat"),
            P("blk", None, None, None, None),
            P("blk", None, None),
            P("blk", None, None),
            P("blk", None),
            P("blk", "feat"),
        ),
        out_specs=(P("blk", "feat"), P("blk", "feat"), P("blk", "feat")),
        check_vma=False,
    )
```

```python
import functools

import jax
import jax.numpy as jnp
from jax import lax
from jax.experimental import pallas as pl
from jax.experimental.pallas import tpu as pltpu
from jax.sharding import PartitionSpec as P

F32 = jnp.float32
BF = jnp.bfloat16
MESH = pl.DeviceIdType.MESH
NB = 128
NZ, NY, NX, NC = 8, 2, 4, 2
N = 512
W = 512
TILE = 128
XCH = 2
XW = W // XCH
RCH = 4
PWHEN = 0
SPLIT = 3
RW = N // RCH
SUB = 256


def dot(a, b):
    return jnp.dot(a, b, preferred_element_type=F32)


def dot_tn(a, b):
    return lax.dot_general(a, b, (((0,), (0,)), ((), ())), preferred_element_type=F32)


def dot_nt(a, b):
    return lax.dot_general(a, b, (((1,), (1,)), ((), ())), preferred_element_type=F32)


def fold(v):
    return jnp.concatenate([v[..., : W // 2], v[..., W // 2 :]], axis=-2)


def loop(count, body):
    def step(i, carry):
        body(i)
        return carry

    lax.fori_loop(0, count, step, 0)


def span(i, size):
    return pl.ds(pl.multiple_of(i * size, size), size)


class Sems:
    def __init__(self, send, recv):
        self.send, self.recv, self.used = send, recv, 0

    def make(self, src, dst, device):
        i = self.used
        self.used += 1
        return pltpu.make_async_remote_copy(
            src_ref=src,
            dst_ref=dst,
            send_sem=self.send.at[i],
            recv_sem=self.recv.at[i],
            device_id=device,
            device_id_type=MESH,
        )

    def choose(self, first, src, other, dst, device, other_device):
        made = self.make(src, dst, device)
        self.used -= 1
        turned = self.make(other, dst, other_device)
        pl.when(first)(lambda: made.start())
        pl.when(jnp.logical_not(first))(lambda: turned.start())
        return made

    def copy(self, src, dst, device):
        made = self.make(src, dst, device)
        made.start()
        return made


class Swap:
    def __init__(self, sems, edge, lo, hi, way, peer, turn, onward):
        self.edge = edge
        self.lo = sems.copy(lo[0], lo[1], peer)
        self.straight = sems.make(hi[0], hi[1], peer)
        self.out = sems.make(hi[0], way, turn)
        self.on = sems.make(way, hi[2], onward)
        self.pick(self.out.start, self.straight.start)

    def pick(self, at_edge, inside):
        pl.when(self.edge)(lambda: at_edge())
        pl.when(jnp.logical_not(self.edge))(lambda: inside())

    def pass_on(self):
        @pl.when(jnp.logical_not(self.edge))
        def _():
            self.out.wait_recv()
            self.on.start()

    def wait_recv(self):
        self.pass_on()
        self.lo.wait_recv()
        self.pick(self.on.wait_recv, self.straight.wait_recv)

    def wait_send(self):
        self.lo.wait_send()

        def inside():
            self.straight.wait_send()
            self.on.wait_send()

        self.pick(self.out.wait_send, inside)


NREMOTE = 112


def kernel(
    x_h, win_h, wout_h, tiles_h, rows_h, cols_h, cnts_h, cot_h,
    out_h, gin_h, gout_h,
    rows, cols, cnts, out_o, gin_o, gout_o,
    x, win, wout, tiles, cot,
    a, xg, sacc, sfull, pre, hfull, dact, zacc, z, z2, zg,
    pbuf, pr, cacc, cfull, wq, bp, oacc, sway,
    g1, g1c, g1r1, g1x, g1r2f, g1r2, g1l,
    g2, g2c, g2r1, g2x, g2r2f, g2r2, g2l,
    lsem, ssem, rsem,
):
    b = lax.axis_index("blk")
    f = lax.axis_index("feat")
    c = lax.rem(b, NC)
    ix = lax.rem(b // NC, NX)
    iy = lax.rem(b // (NC * NX), NY)
    iz = b // (NC * NX * NY)
    nf = 1 - f
    nc = 1 - c

    def node(zz, yy, xx, cc):
        return (((zz * NY + yy) * NX + xx) * NC + cc, f)

    def near(o):
        return (lax.rem(b + o + NB, NB), f)

    peer = (b, nf)
    edge = jnp.logical_or(ix == 0, ix == NX - 1)
    beside = ix + 1 - 2 * lax.rem(ix, 2)
    beside_node = (((iz * NY + iy) * NX + beside) * NC + c)
    turn, onward = (beside_node, nf), (beside_node, f)
    across = (((iz * NY + 1 - iy) * NX + ix) * NC + c, nf)
    partner = node(iz, iy, ix, nc)
    xpeers = [lax.rem(ix + d, NX) for d in range(1, NX)]
    zpeers = [lax.rem(iz + d, NZ) for d in range(1, NZ)]
    ypeer = 1 - iy

    greeted = [near(2), near(-2), peer, partner, turn, across]
    greeted += [node(iz, iy, xx, c) for xx in xpeers]
    greeted += [node(zz, iy, ix, c) for zz in zpeers]
    greeted += [node(zz, ypeer, ix, c) for zz in [iz] + zpeers]

    barrier = pltpu.get_barrier_semaphore()
    for device in greeted:
        pl.semaphore_signal(barrier, inc=1, device_id=device, device_id_type=MESH)

    @pl.when(ix == 0)
    def _():
        pl.semaphore_signal(
            barrier, inc=1, device_id=(near(-2)[0], nf), device_id_type=MESH
        )

    @pl.when(ix == NX - 1)
    def _():
        pl.semaphore_signal(barrier, inc=1, device_id=(near(2)[0], nf), device_id_type=MESH)

    loads = []
    for i, (src, dst) in enumerate(
        ((x_h, x), (tiles_h, tiles), (cot_h, cot), (win_h, win), (wout_h, wout),
         (rows_h, rows), (cols_h, cols), (cnts_h, cnts))
    ):
        made = pltpu.make_async_copy(src, dst, lsem.at[i])
        made.start()
        loads.append(made)
    loads[0].wait()
    pl.semaphore_wait(barrier, len(greeted) + edge.astype(jnp.int32))

    sems = Sems(ssem, rsem)
    step_of = (0, 4, 3 - 2 * c, 1 + 2 * c)

    def swap(ref, out_slot, in_slot, start, size, cs, way):
        near_rows = size * SPLIT // 4
        lo, hi = pl.ds(start, near_rows), pl.ds(start + near_rows, size - near_rows)
        return Swap(
            sems, edge,
            (ref(out_slot, lo, cs), ref(in_slot[0], lo, cs)),
            (ref(out_slot, hi, cs), ref(in_slot[0], hi, cs), ref(in_slot[1], hi, cs)),
            way, peer, turn, onward,
        )

    def spread(src, dst):
        return [
            sems.copy(src, dst(0), near(2)),
            sems.copy(src, dst(1), near(-2)),
            sems.copy(src, dst(2), partner),
        ]

    def on_side(copies, side):
        @pl.when(side == 0)
        def _():
            copies[0].wait_recv()

        @pl.when(side == 1)
        def _():
            copies[1].wait_recv()

    xcopies = []
    for j in range(XCH):
        cs = pl.ds(j * XW, XW)
        xcopies.append(spread(x.at[:, cs], lambda i, cs=cs: xg.at[i, :, cs]))

    for i in (1, 5, 6, 7):
        loads[i].wait()

    def densify(s):
        live = cnts[0, s]
        place = [
            jnp.where(k < live, rows[s, 0, k] * 4 + cols[s, 0, k], -1) for k in range(8)
        ]
        for r in range(4):
            for q in range(4):
                block = jnp.zeros((TILE, TILE), BF)
                for k in range(8):
                    block = lax.select(place[k] == r * 4 + q, tiles[s, k], block)
                a[s, r * TILE : (r + 1) * TILE, q * TILE : (q + 1) * TILE] = block

    loop(5, densify)
    loads[2].wait()

    def own_s(i):
        sacc[span(i, SUB), :] = dot(a[2, span(i, SUB), :], x[...])

    loop(N // SUB, own_s)


    def product(slot, step, helped):
        def rows_of(k):
            rs = span(k, SUB)
            part = dot_tn(a[step, :, rs], cot[...])
            if helped:
                part += pr[3, rs, :].astype(F32)
            pbuf[slot, rs, :] = part.astype(BF)

        loop(N // SUB, rows_of)

    product(2, step_of[2], False)
    pcopies = [sems.copy(pbuf.at[2], pr.at[2], partner)]
    product(3, step_of[3], False)
    help_copy = sems.copy(pbuf.at[3], pr.at[3], partner)
    product(c, 4 * c, False)

    def own_c(k):
        cacc[span(k, SUB), :] = dot_tn(a[2, :, span(k, SUB)], cot[...])

    loop(N // SUB, own_c)
    help_copy.wait_recv()
    product(nc, 4 * nc, True)

    def send_products():
        pcopies.append(sems.copy(pbuf.at[c], pr.at[c], near(4 * c - 2)))
        pcopies.append(sems.copy(pbuf.at[nc], pr.at[nc], near(4 * nc - 2)))

    if PWHEN == 0:
        send_products()
    scopies = []
    relays = []
    for j in range(XCH):
        cs = pl.ds(j * XW, XW)

        def add(i, last=False):
            def rows_of(k):
                rs = span(k, SUB)
                total = sacc[rs, cs] + dot(a[step_of[i], rs, :], xg[i, :, cs])
                if last:
                    sfull[f, rs, cs] = total.astype(BF)
                else:
                    sacc[rs, cs] = total

            loop(N // SUB, rows_of)

        xcopies[j][2].wait_recv()
        add(2)
        on_side(xcopies[j], nc)
        relay = sems.copy(xg.at[nc, :, cs], xg.at[3, :, cs], partner)
        relays.append(relay)
        on_side(xcopies[j], c)
        add(0)
        add(1)
        relay.wait_recv()
        add(3, True)
        scopies.append(
            swap(lambda i, r, q: sfull.at[i, r, q], f, (f, nf), 0, N, cs, sway.at[:, cs])
        )
    if PWHEN == 1:
        send_products()

    loads[4].wait()
    half = pl.ds(pl.multiple_of(c * (N // 2), N // 2), N // 2)
    wqcopy = [
        sems.copy(wout.at[nf, half, :], wq.at[0, half, :], across),
        sems.copy(wout.at[f, half, :], wq.at[1, half, :], across),
    ]
    loads[3].wait()

    def pre_own(k):
        rs = span(k, SUB)
        pre[rs, :] = dot(sfull[f, rs, :], win[f])

    loop(N // SUB, pre_own)
    for j in range(XCH - 1):
        cs = pl.ds(j * XW, XW)
        scopies[j].wait_recv()

        def pre_add(k):
            rs = span(k, SUB)
            pre[rs, :] += dot(sfull[nf, rs, cs], win[nf, cs, :])

        loop(N // SUB, pre_add)
    cs = pl.ds((XCH - 1) * XW, XW)
    scopies[-1].wait_recv()
    if PWHEN == 2:
        send_products()
    hcopies = []

    def hidden_piece(j):

        def act(k):
            rs = pl.ds(pl.multiple_of(j * RW + k * TILE, TILE), TILE)
            v = pre[rs, :] + dot(sfull[nf, rs, cs], win[nf, cs, :])
            g = 1.0 / (1.0 + jnp.exp(-v))
            hfull[f, rs, :] = (v * g).astype(BF)
            dact[rs, :] = g * (1.0 + v * (1.0 - g))

        loop(RW // TILE, act)
        rs = pl.ds(j * RW, RW)
        hcopies.append(sems.copy(hfull.at[f, rs, :], hfull.at[f, rs, :], peer))

    hidden_piece(0)
    hidden_piece(1)
    hidden_piece(2)
    hidden_piece(3)
    for copy in pcopies:
        copy.wait_recv()

    def close_c(k):
        rs = span(k, TILE)
        total = cacc[rs, :]
        for i in range(3):
            total += pr[i, rs, :].astype(F32)
        cfull[f, rs, :] = total.astype(BF)

    loop(N // TILE, close_c)

    ccopy = sems.copy(cfull.at[f], cfull.at[f], peer)

    def z_own(k):
        rs = span(k, SUB)
        zacc[rs, :] = dot(hfull[f, rs, :], wout[f])

    loop(N // SUB, z_own)
    wqpass = []
    for i in range(2):
        wqcopy[i].wait_recv()
        wqpass.append(sems.copy(wq.at[i, half, :], wq.at[i, half, :], partner))


    def gout_rows(side):
        def rows_of(k):
            part = dot_tn(hfull[side, :, span(k, TILE)], cfull[f])
            g1[side * 4 + k] = part.reshape(NY, NX, NC, 8, W)

        loop(4, rows_of)

    def side_of(ref, side, *rest):
        return ref.at[(pl.ds(side * 4, 4), *rest)]

    def to_partner(g, gc, side):
        return sems.copy(
            side_of(g, side, slice(None), slice(None), nc), side_of(gc, side), partner
        )

    def across_x(copy, g, gc, r1, gx, side):
        copy.wait_recv()

        def first(k):
            i = side * 4 + k
            r1[i] = fold(g[i, :, :, c] + gc[i]).astype(BF)

        loop(4, first)
        return [
            sems.copy(
                side_of(r1, side, slice(None), xx), gx.at[d, pl.ds(side * 4, 4)],
                node(iz, iy, xx, c),
            )
            for d, xx in enumerate(xpeers)
        ]

    gout_rows(f)
    g1core = [to_partner(g1, g1c, f)]

    def bh_own(k):
        rs = span(k, SUB)
        cacc[rs, :] = dot_nt(cfull[f, rs, :], wout[f])

    loop(N // SUB, bh_own)
    for copy in wqpass:
        copy.wait_recv()
    g1xc = across_x(g1core[0], g1, g1c, g1r1, g1x, f)
    zcopies = []

    def z_piece(j):
        hcopies[j].wait_recv()
        rs = pl.ds(j * RW, RW)
        z[rs, :] = (zacc[rs, :] + dot(hfull[nf, rs, :], wout[nf])).astype(BF)

        @pl.when(edge)
        def _():
            z2[rs, :] = (
                dot(hfull[f, rs, :], wq[0]) + dot(hfull[nf, rs, :], wq[1])
            ).astype(BF)

        mine, turned = z.at[rs, :], z2.at[rs, :]
        zcopies.append([
            sems.choose(ix != NX - 1, mine, turned, zg.at[0, rs, :], near(2), (near(2)[0], nf)),
            sems.choose(ix != 0, mine, turned, zg.at[1, rs, :], near(-2), (near(-2)[0], nf)),
            sems.copy(mine, zg.at[2, rs, :], partner),
        ])

    z_piece(0)
    z_piece(1)
    z_piece(2)
    z_piece(3)
    gout_rows(nf)
    g1core.append(to_partner(g1, g1c, nf))
    def own_o(k):
        rs = span(k, SUB)
        oacc[rs, :] = dot(a[2, rs, :], z[...])

    loop(N // SUB, own_o)
    g1xc += across_x(g1core[1], g1, g1c, g1r1, g1x, nf)

    def second(g, gc, gx, r2f, r2):
        def part(k):
            total = fold(g[k, :, ix, c] + gc[k, :, ix])
            for d in range(NX - 1):
                total += gx[d, k].astype(F32)
            r2f[k] = total
            r2[k] = total.astype(BF)

        loop(NZ, part)

    stores = []

    def relay_part(part):
        made = []
        for j in range(part * RCH // 2, (part + 1) * RCH // 2):
            ks = pl.ds(j * RW, RW)
            on_side(zcopies[j], nc)
            made.append(sems.copy(zg.at[nc, ks, :], zg.at[3, ks, :], partner))
            zcopies[j][2].wait_recv()
            on_side(zcopies[j], c)
        relays.extend(made)
        return made

    def out_part(made, part):
        ks = pl.ds(part * (N // 2), N // 2)

        def direct(k):
            rs = span(k, SUB)
            total = oacc[rs, :]
            for i in range(3):
                total += dot(a[step_of[i], rs, ks], zg[i, ks, :])
            oacc[rs, :] = total

        loop(N // SUB, direct)
        for copy in made:
            copy.wait_recv()
        for k in range(N // SUB):
            rs = pl.ds(k * SUB, SUB)
            total = oacc[rs, :] + dot(a[step_of[3], rs, ks], zg[3, ks, :])
            if part == 0:
                oacc[rs, :] = total
            else:
                out_o[rs, :] = total.astype(BF)
                stores.append(
                    pltpu.make_async_copy(out_o.at[rs, :], out_h.at[rs, :], lsem.at[10 + k])
                )
                stores[-1].start()


    far = [
        (zz, yy) for zz in [iz] + zpeers for yy in (iy, ypeer)
    ][1:]

    def second(copies, g, gc, gx, r2f, r2, gl):
        for copy in copies:
            copy.wait_recv()

        def part(k):
            total = fold(g[k, :, ix, c] + gc[k, :, ix])
            for d in range(NX - 1):
                total += gx[d, k].astype(F32)
            r2f[k] = total
            r2[k] = total.astype(BF)

        loop(NZ, part)
        return [
            sems.copy(r2.at[zz, yy], gl.at[d], node(zz, yy, ix, c))
            for d, (zz, yy) in enumerate(far)
        ]

    def last(copies, r2f, gl, to, into, i):
        for copy in copies:
            copy.wait_recv()
        total = r2f[iz, iy]
        for d in range(len(far)):
            total += gl[d].astype(F32)
        to[:, : W // 2] = total[:8]
        to[:, W // 2 :] = total[8:]
        stores.append(pltpu.make_async_copy(to, into, lsem.at[i]))
        stores[-1].start()

    part0 = relay_part(0)
    out_part(part0, 0)
    g1last = second(g1xc, g1, g1c, g1x, g1r2f, g1r2, g1l)
    ccopy.wait_recv()

    def close_bp(k):
        rs = span(k, SUB)
        back = cacc[rs, :] + dot_nt(cfull[nf, rs, :], wq[0])
        bp[rs, :] = (back * dact[rs, :]).astype(BF)

    loop(N // SUB, close_bp)
    g2core = []
    for side in range(2):

        def gin_rows(k, side=side):
            part = dot_tn(sfull[side, :, span(k, TILE)], bp[...])
            g2[side * 4 + k] = part.reshape(NY, NX, NC, 8, W)

        loop(4, gin_rows)
        g2core.append(to_partner(g2, g2c, side))
    g2xc = []
    for side in range(2):
        g2xc += across_x(g2core[side], g2, g2c, g2r1, g2x, side)
    part1 = relay_part(1)
    out_part(part1, 1)
    last(g1last, g1r2f, g1l, gout_o, gout_h, 9)
    g2last = second(g2xc, g2, g2c, g2x, g2r2f, g2r2, g2l)
    last(g2last, g2r2f, g2l, gin_o, gin_h, 8)

    sent = [copy for group in xcopies + zcopies for copy in group] + pcopies + scopies + hcopies + relays
    sent += [help_copy, ccopy] + g2core + g1core + wqcopy + wqpass
    sent += g1xc + g2xc + g1last + g2last
    for copy in stores:
        copy.wait()
    for copy in sent:
        copy.wait_send()


def hand_over(a_ref, b_ref, c_ref, a_o, b_o, c_o, a_v, b_v, c_v, insem, outsem):
    moves = [(b_ref, b_v, b_o), (c_ref, c_v, c_o)]
    for k in range(4):
        rs = pl.ds(k * (N // 4), N // 4)
        moves.append((a_ref.at[rs, :], a_v.at[rs, :], a_o.at[rs, :]))
    taken = [pltpu.make_async_copy(m[0], m[1], insem.at[i]) for i, m in enumerate(moves)]
    given = [pltpu.make_async_copy(m[1], m[2], outsem.at[i]) for i, m in enumerate(moves)]
    for copy in taken:
        copy.start()
    for into, out in zip(taken, given):
        into.wait()
        out.start()
    for copy in given:
        copy.wait()


def shards(features, weight_in, weight_out, adj_tiles, tile_rows, tile_cols, tile_counts, cotangent):
    anyspace = pl.BlockSpec(memory_space=pl.ANY)
    V = pltpu.VMEM
    scratch = [
        pltpu.SMEM((5, 1, 8), jnp.int32), pltpu.SMEM((5, 1, 8), jnp.int32), pltpu.SMEM((1, 5), jnp.int32),
        V((N, W), BF), V((8, W), F32), V((8, W), F32),
        V((N, W), BF), V((2, 512, W), BF), V((2, 512, W), BF), V((5, 8, TILE, TILE), BF), V((N, W), BF),
        V((5, N, N), BF), V((4, N, W), BF), V((N, W), F32), V((2, N, W), BF), V((N, W), F32),
        V((2, N, W), BF), V((N, W), F32), V((N, W), F32), V((N, W), BF), V((N, W), BF), V((4, N, W), BF),
        V((4, N, W), BF), V((4, N, W), BF), V((N, W), F32), V((2, N, W), BF), V((2, N, W), BF),
        V((N, W), BF), V((N, W), F32), V((N - N * SPLIT // 4, W), BF),
        V((NZ, NY, NX, NC, 8, W), F32), V((NZ, NY, NX, 8, W), F32), V((NZ, NY, NX, 16, W // 2), BF),
        V((3, NZ, NY, 16, W // 2), BF), V((NZ, NY, 16, W // 2), F32), V((NZ, NY, 16, W // 2), BF),
        V((15, 16, W // 2), BF),
        V((NZ, NY, NX, NC, 8, W), F32), V((NZ, NY, NX, 8, W), F32), V((NZ, NY, NX, 16, W // 2), BF),
        V((3, NZ, NY, 16, W // 2), BF), V((NZ, NY, 16, W // 2), F32), V((NZ, NY, 16, W // 2), BF),
        V((15, 16, W // 2), BF),
        pltpu.SemaphoreType.DMA((8 + 2 + N // SUB,)),
        pltpu.SemaphoreType.DMA((NREMOTE,)),
        pltpu.SemaphoreType.DMA((NREMOTE,)),
    ]
    results = pl.pallas_call(
        kernel,
        out_shape=(
            jax.ShapeDtypeStruct((N, W), BF),
            jax.ShapeDtypeStruct((8, W), F32),
            jax.ShapeDtypeStruct((8, W), F32),
        ),
        in_specs=[anyspace] * 8,
        out_specs=(anyspace,) * 3,
        scratch_shapes=scratch,
        compiler_params=pltpu.CompilerParams(
            collective_id=0, has_side_effects=True, vmem_limit_bytes=60 * 1024 * 1024
        ),
        name="graph_layers",
    )(
        features,
        weight_in.reshape(2, 512, W),
        weight_out.reshape(2, 512, W),
        adj_tiles.reshape(5, 8, TILE, TILE),
        tile_rows.transpose(1, 0, 2),
        tile_cols.transpose(1, 0, 2),
        tile_counts,
        cotangent,
    )
    return pl.pallas_call(
        hand_over,
        out_shape=tuple(jax.ShapeDtypeStruct(r.shape, r.dtype) for r in results),
        in_specs=[anyspace] * 3,
        out_specs=[anyspace] * 3,
        scratch_shapes=[
            V((N, W), BF), V((8, W), F32), V((8, W), F32),
            pltpu.SemaphoreType.DMA((6,)), pltpu.SemaphoreType.DMA((6,)),
        ],
        name="hand_over",
    )(*results)


def solution(mesh):
    return jax.shard_map(
        shards,
        mesh=mesh,
        in_specs=(
            P("blk", "feat"),
            P(None, "feat"),
            P(None, "feat"),
            P("blk", None, None, None, None),
            P("blk", None, None),
            P("blk", None, None),
            P("blk", None),
            P("blk", "feat"),
        ),
        out_specs=(P("blk", "feat"), P("blk", "feat"), P("blk", "feat")),
        check_vma=False,
    )
```

```python
import functools

import jax
import jax.numpy as jnp
from jax import lax
from jax.experimental import pallas as pl
from jax.experimental.pallas import tpu as pltpu
from jax.sharding import PartitionSpec as P

F32 = jnp.float32
BF = jnp.bfloat16
MESH = pl.DeviceIdType.MESH
NB = 128
NZ, NY, NX, NC = 8, 2, 4, 2
N = 512
W = 512
TILE = 128
XCH = 2
XW = W // XCH
RCH = 4
PWHEN = 0
SPLIT = 5
CSPLIT = 6
RW = N // RCH
SUB = 256


def dot(a, b):
    return jnp.dot(a, b, preferred_element_type=F32)


def dot_tn(a, b):
    return lax.dot_general(a, b, (((0,), (0,)), ((), ())), preferred_element_type=F32)


def dot_nt(a, b):
    return lax.dot_general(a, b, (((1,), (1,)), ((), ())), preferred_element_type=F32)


def fold(v):
    return jnp.concatenate([v[..., : W // 2], v[..., W // 2 :]], axis=-2)


def loop(count, body):
    def step(i, carry):
        body(i)
        return carry

    lax.fori_loop(0, count, step, 0)


def span(i, size):
    return pl.ds(pl.multiple_of(i * size, size), size)


class Sems:
    def __init__(self, send, recv):
        self.send, self.recv, self.used = send, recv, 0

    def make(self, src, dst, device):
        i = self.used
        self.used += 1
        return pltpu.make_async_remote_copy(
            src_ref=src,
            dst_ref=dst,
            send_sem=self.send.at[i],
            recv_sem=self.recv.at[i],
            device_id=device,
            device_id_type=MESH,
        )

    def choose(self, first, src, other, dst, device, other_device):
        made = self.make(src, dst, device)
        self.used -= 1
        turned = self.make(other, dst, other_device)
        pl.when(first)(lambda: made.start())
        pl.when(jnp.logical_not(first))(lambda: turned.start())
        return made

    def copy(self, src, dst, device):
        made = self.make(src, dst, device)
        made.start()
        return made


class Swap:
    def __init__(self, sems, edge, lo, hi, way, peer, turn, onward):
        self.edge = edge
        self.lo = sems.copy(lo[0], lo[1], peer)
        self.straight = sems.make(hi[0], hi[1], peer)
        self.out = sems.make(hi[0], way, turn)
        self.on = sems.make(way, hi[2], onward)
        self.pick(self.out.start, self.straight.start)

    def pick(self, at_edge, inside):
        pl.when(self.edge)(lambda: at_edge())
        pl.when(jnp.logical_not(self.edge))(lambda: inside())

    def pass_on(self):
        @pl.when(jnp.logical_not(self.edge))
        def _():
            self.out.wait_recv()
            self.on.start()

    def wait_recv(self):
        self.lo.wait_recv()
        self.pick(self.on.wait_recv, self.straight.wait_recv)

    def wait_send(self):
        self.lo.wait_send()

        def inside():
            self.straight.wait_send()
            self.on.wait_send()

        self.pick(self.out.wait_send, inside)


NREMOTE = 112


def kernel(
    x_h, win_h, wout_h, tiles_h, rows_h, cols_h, cnts_h, cot_h,
    out_h, gin_h, gout_h,
    rows, cols, cnts, out_o, gin_o, gout_o,
    x, win, wout, tiles, cot,
    a, xg, sacc, sfull, pre, hfull, dact, zacc, z, z2, zg,
    pbuf, pr, cacc, cfull, wq, bp, oacc, sway, cway,
    g1, g1c, g1r1, g1x, g1r2f, g1r2, g1l,
    g2, g2c, g2r1, g2x, g2r2f, g2r2, g2l,
    lsem, ssem, rsem,
):
    b = lax.axis_index("blk")
    f = lax.axis_index("feat")
    c = lax.rem(b, NC)
    ix = lax.rem(b // NC, NX)
    iy = lax.rem(b // (NC * NX), NY)
    iz = b // (NC * NX * NY)
    nf = 1 - f
    nc = 1 - c

    def node(zz, yy, xx, cc):
        return (((zz * NY + yy) * NX + xx) * NC + cc, f)

    def near(o):
        return (lax.rem(b + o + NB, NB), f)

    peer = (b, nf)
    edge = jnp.logical_or(ix == 0, ix == NX - 1)
    beside = ix + 1 - 2 * lax.rem(ix, 2)
    beside_node = (((iz * NY + iy) * NX + beside) * NC + c)
    turn, onward = (beside_node, nf), (beside_node, f)
    across = (((iz * NY + 1 - iy) * NX + ix) * NC + c, nf)
    partner = node(iz, iy, ix, nc)
    xpeers = [lax.rem(ix + d, NX) for d in range(1, NX)]
    zpeers = [lax.rem(iz + d, NZ) for d in range(1, NZ)]
    ypeer = 1 - iy

    greeted = [near(2), near(-2), peer, partner, turn, across]
    greeted += [node(iz, iy, xx, c) for xx in xpeers]
    greeted += [node(zz, iy, ix, c) for zz in zpeers]
    greeted += [node(zz, ypeer, ix, c) for zz in [iz] + zpeers]

    barrier = pltpu.get_barrier_semaphore()
    for device in greeted:
        pl.semaphore_signal(barrier, inc=1, device_id=device, device_id_type=MESH)

    @pl.when(ix == 0)
    def _():
        pl.semaphore_signal(
            barrier, inc=1, device_id=(near(-2)[0], nf), device_id_type=MESH
        )

    @pl.when(ix == NX - 1)
    def _():
        pl.semaphore_signal(barrier, inc=1, device_id=(near(2)[0], nf), device_id_type=MESH)

    loads = []
    for i, (src, dst) in enumerate(
        ((x_h, x), (tiles_h, tiles), (cot_h, cot), (win_h, win), (wout_h, wout),
         (rows_h, rows), (cols_h, cols), (cnts_h, cnts))
    ):
        made = pltpu.make_async_copy(src, dst, lsem.at[i])
        made.start()
        loads.append(made)
    loads[0].wait()
    pl.semaphore_wait(barrier, len(greeted) + edge.astype(jnp.int32))

    sems = Sems(ssem, rsem)
    step_of = (0, 4, 3 - 2 * c, 1 + 2 * c)

    def swap(ref, out_slot, in_slot, start, size, cs, way, split):
        near_rows = size * split // 8
        lo, hi = pl.ds(start, near_rows), pl.ds(start + near_rows, size - near_rows)
        return Swap(
            sems, edge,
            (ref(out_slot, lo, cs), ref(in_slot[0], lo, cs)),
            (ref(out_slot, hi, cs), ref(in_slot[0], hi, cs), ref(in_slot[1], hi, cs)),
            way, peer, turn, onward,
        )

    def spread(src, dst):
        return [
            sems.copy(src, dst(0), near(2)),
            sems.copy(src, dst(1), near(-2)),
            sems.copy(src, dst(2), partner),
        ]

    def on_side(copies, side):
        @pl.when(side == 0)
        def _():
            copies[0].wait_recv()

        @pl.when(side == 1)
        def _():
            copies[1].wait_recv()

    xcopies = []
    for j in range(XCH):
        cs = pl.ds(j * XW, XW)
        xcopies.append(spread(x.at[:, cs], lambda i, cs=cs: xg.at[i, :, cs]))

    for i in (1, 5, 6, 7):
        loads[i].wait()

    def densify(s):
        live = cnts[0, s]
        place = [
            jnp.where(k < live, rows[s, 0, k] * 4 + cols[s, 0, k], -1) for k in range(8)
        ]
        for r in range(4):
            for q in range(4):
                block = jnp.zeros((TILE, TILE), BF)
                for k in range(8):
                    block = lax.select(place[k] == r * 4 + q, tiles[s, k], block)
                a[s, r * TILE : (r + 1) * TILE, q * TILE : (q + 1) * TILE] = block

    loop(5, densify)
    loads[2].wait()

    def own_s(i):
        sacc[span(i, SUB), :] = dot(a[2, span(i, SUB), :], x[...])

    loop(N // SUB, own_s)


    def product(slot, step, helped):
        def rows_of(k):
            rs = span(k, SUB)
            part = dot_tn(a[step, :, rs], cot[...])
            if helped:
                part += pr[3, rs, :].astype(F32)
            pbuf[slot, rs, :] = part.astype(BF)

        loop(N // SUB, rows_of)

    product(2, step_of[2], False)
    pcopies = [sems.copy(pbuf.at[2], pr.at[2], partner)]
    product(3, step_of[3], False)
    help_copy = sems.copy(pbuf.at[3], pr.at[3], partner)
    product(c, 4 * c, False)

    def own_c(k):
        cacc[span(k, SUB), :] = dot_tn(a[2, :, span(k, SUB)], cot[...])

    loop(N // SUB, own_c)
    help_copy.wait_recv()
    product(nc, 4 * nc, True)

    def send_products():
        pcopies.append(sems.copy(pbuf.at[c], pr.at[c], near(4 * c - 2)))
        pcopies.append(sems.copy(pbuf.at[nc], pr.at[nc], near(4 * nc - 2)))

    if PWHEN == 0:
        send_products()
    scopies = []
    relays = []
    for j in range(XCH):
        cs = pl.ds(j * XW, XW)

        def add(i, last=False):
            def rows_of(k):
                rs = span(k, SUB)
                total = sacc[rs, cs] + dot(a[step_of[i], rs, :], xg[i, :, cs])
                if last:
                    sfull[f, rs, cs] = total.astype(BF)
                else:
                    sacc[rs, cs] = total

            loop(N // SUB, rows_of)

        xcopies[j][2].wait_recv()
        add(2)
        on_side(xcopies[j], nc)
        relay = sems.copy(xg.at[nc, :, cs], xg.at[3, :, cs], partner)
        relays.append(relay)
        on_side(xcopies[j], c)
        add(0)
        add(1)
        relay.wait_recv()
        add(3, True)
        scopies.append(
            swap(lambda i, r, q: sfull.at[i, r, q], f, (f, nf), 0, N, cs, sway.at[:, cs], SPLIT)
        )
    if PWHEN == 1:
        send_products()

    loads[4].wait()
    half = pl.ds(pl.multiple_of(c * (N // 2), N // 2), N // 2)
    wqcopy = [
        sems.copy(wout.at[nf, half, :], wq.at[0, half, :], across),
        sems.copy(wout.at[f, half, :], wq.at[1, half, :], across),
    ]
    loads[3].wait()

    def pre_own(k):
        rs = span(k, SUB)
        pre[rs, :] = dot(sfull[f, rs, :], win[f])

    loop(N // SUB, pre_own)
    for j in range(XCH - 1):
        cs = pl.ds(j * XW, XW)
        scopies[j].pass_on()
        scopies[j].wait_recv()

        def pre_add(k):
            rs = span(k, SUB)
            pre[rs, :] += dot(sfull[nf, rs, cs], win[nf, cs, :])

        loop(N // SUB, pre_add)
    cs = pl.ds((XCH - 1) * XW, XW)
    scopies[-1].pass_on()
    scopies[-1].wait_recv()
    if PWHEN == 2:
        send_products()
    hcopies = []

    def hidden_piece(j):

        def act(k):
            rs = pl.ds(pl.multiple_of(j * RW + k * TILE, TILE), TILE)
            v = pre[rs, :] + dot(sfull[nf, rs, cs], win[nf, cs, :])
            g = 1.0 / (1.0 + jnp.exp(-v))
            hfull[f, rs, :] = (v * g).astype(BF)
            dact[rs, :] = g * (1.0 + v * (1.0 - g))

        loop(RW // TILE, act)
        rs = pl.ds(j * RW, RW)
        hcopies.append(sems.copy(hfull.at[f, rs, :], hfull.at[f, rs, :], peer))

    hidden_piece(0)
    hidden_piece(1)
    hidden_piece(2)
    hidden_piece(3)
    for copy in pcopies:
        copy.wait_recv()

    def close_c(k):
        rs = span(k, TILE)
        total = cacc[rs, :]
        for i in range(3):
            total += pr[i, rs, :].astype(F32)
        cfull[f, rs, :] = total.astype(BF)

    loop(N // TILE, close_c)

    ccopy = swap(
        lambda i, r, q: cfull.at[i, r, q], f, (f, nf), 0, N, pl.ds(0, W), cway, CSPLIT
    )

    def z_own(k):
        rs = span(k, SUB)
        zacc[rs, :] = dot(hfull[f, rs, :], wout[f])

    loop(N // SUB, z_own)
    wqpass = []
    for i in range(2):
        wqcopy[i].wait_recv()
        wqpass.append(sems.copy(wq.at[i, half, :], wq.at[i, half, :], partner))


    def gout_rows(side):
        def rows_of(k):
            part = dot_tn(hfull[side, :, span(k, TILE)], cfull[f])
            g1[side * 4 + k] = part.reshape(NY, NX, NC, 8, W)

        loop(4, rows_of)

    def side_of(ref, side, *rest):
        return ref.at[(pl.ds(side * 4, 4), *rest)]

    def to_partner(g, gc, side):
        return sems.copy(
            side_of(g, side, slice(None), slice(None), nc), side_of(gc, side), partner
        )

    def across_x(copy, g, gc, r1, gx, side):
        copy.wait_recv()

        def first(k):
            i = side * 4 + k
            r1[i] = fold(g[i, :, :, c] + gc[i]).astype(BF)

        loop(4, first)
        return [
            sems.copy(
                side_of(r1, side, slice(None), xx), gx.at[d, pl.ds(side * 4, 4)],
                node(iz, iy, xx, c),
            )
            for d, xx in enumerate(xpeers)
        ]

    gout_rows(f)
    g1core = [to_partner(g1, g1c, f)]

    def bh_own(k):
        rs = span(k, SUB)
        cacc[rs, :] = dot_nt(cfull[f, rs, :], wout[f])

    loop(N // SUB, bh_own)
    for copy in wqpass:
        copy.wait_recv()
    g1xc = across_x(g1core[0], g1, g1c, g1r1, g1x, f)
    zcopies = []

    def z_piece(j):
        hcopies[j].wait_recv()
        rs = pl.ds(j * RW, RW)
        z[rs, :] = (zacc[rs, :] + dot(hfull[nf, rs, :], wout[nf])).astype(BF)

        @pl.when(edge)
        def _():
            z2[rs, :] = (
                dot(hfull[f, rs, :], wq[0]) + dot(hfull[nf, rs, :], wq[1])
            ).astype(BF)

        mine, turned = z.at[rs, :], z2.at[rs, :]
        zcopies.append([
            sems.choose(ix != NX - 1, mine, turned, zg.at[0, rs, :], near(2), (near(2)[0], nf)),
            sems.choose(ix != 0, mine, turned, zg.at[1, rs, :], near(-2), (near(-2)[0], nf)),
            sems.copy(mine, zg.at[2, rs, :], partner),
        ])

    z_piece(0)
    z_piece(1)
    z_piece(2)
    z_piece(3)
    gout_rows(nf)
    g1core.append(to_partner(g1, g1c, nf))
    def own_o(k):
        rs = span(k, SUB)
        oacc[rs, :] = dot(a[2, rs, :], z[...])

    loop(N // SUB, own_o)
    g1xc += across_x(g1core[1], g1, g1c, g1r1, g1x, nf)

    def second(g, gc, gx, r2f, r2):
        def part(k):
            total = fold(g[k, :, ix, c] + gc[k, :, ix])
            for d in range(NX - 1):
                total += gx[d, k].astype(F32)
            r2f[k] = total
            r2[k] = total.astype(BF)

        loop(NZ, part)

    stores = []

    def relay_part(part):
        made = []
        for j in range(part * RCH // 2, (part + 1) * RCH // 2):
            ks = pl.ds(j * RW, RW)
            on_side(zcopies[j], nc)
            made.append(sems.copy(zg.at[nc, ks, :], zg.at[3, ks, :], partner))
            zcopies[j][2].wait_recv()
            on_side(zcopies[j], c)
        relays.extend(made)
        return made

    def out_part(made, part):
        ks = pl.ds(part * (N // 2), N // 2)

        def direct(k):
            rs = span(k, SUB)
            total = oacc[rs, :]
            for i in range(3):
                total += dot(a[step_of[i], rs, ks], zg[i, ks, :])
            oacc[rs, :] = total

        loop(N // SUB, direct)
        for copy in made:
            copy.wait_recv()
        for k in range(N // SUB):
            rs = pl.ds(k * SUB, SUB)
            total = oacc[rs, :] + dot(a[step_of[3], rs, ks], zg[3, ks, :])
            if part == 0:
                oacc[rs, :] = total
            else:
                out_o[rs, :] = total.astype(BF)
                stores.append(
                    pltpu.make_async_copy(out_o.at[rs, :], out_h.at[rs, :], lsem.at[10 + k])
                )
                stores[-1].start()


    far = [
        (zz, yy) for zz in [iz] + zpeers for yy in (iy, ypeer)
    ][1:]

    def second(copies, g, gc, gx, r2f, r2, gl):
        for copy in copies:
            copy.wait_recv()

        def part(k):
            total = fold(g[k, :, ix, c] + gc[k, :, ix])
            for d in range(NX - 1):
                total += gx[d, k].astype(F32)
            r2f[k] = total
            r2[k] = total.astype(BF)

        loop(NZ, part)
        return [
            sems.copy(r2.at[zz, yy], gl.at[d], node(zz, yy, ix, c))
            for d, (zz, yy) in enumerate(far)
        ]

    def last(copies, r2f, gl, to, into, i):
        for copy in copies:
            copy.wait_recv()
        total = r2f[iz, iy]
        for d in range(len(far)):
            total += gl[d].astype(F32)
        to[:, : W // 2] = total[:8]
        to[:, W // 2 :] = total[8:]
        stores.append(pltpu.make_async_copy(to, into, lsem.at[i]))
        stores[-1].start()

    ccopy.pass_on()
    part0 = relay_part(0)
    out_part(part0, 0)
    ccopy.wait_recv()

    def close_bp(k):
        rs = span(k, SUB)
        back = cacc[rs, :] + dot_nt(cfull[nf, rs, :], wq[0])
        bp[rs, :] = (back * dact[rs, :]).astype(BF)

    loop(N // SUB, close_bp)
    g2core = []
    for side in range(2):

        def gin_rows(k, side=side):
            part = dot_tn(sfull[side, :, span(k, TILE)], bp[...])
            g2[side * 4 + k] = part.reshape(NY, NX, NC, 8, W)

        loop(4, gin_rows)
        g2core.append(to_partner(g2, g2c, side))
    g2xc = []
    for side in range(2):
        g2xc += across_x(g2core[side], g2, g2c, g2r1, g2x, side)
    g1last = second(g1xc, g1, g1c, g1x, g1r2f, g1r2, g1l)
    part1 = relay_part(1)
    out_part(part1, 1)
    g2last = second(g2xc, g2, g2c, g2x, g2r2f, g2r2, g2l)
    last(g1last, g1r2f, g1l, gout_o, gout_h, 9)
    last(g2last, g2r2f, g2l, gin_o, gin_h, 8)

    sent = [copy for group in xcopies + zcopies for copy in group] + pcopies + scopies + hcopies + relays
    sent += [help_copy, ccopy] + g2core + g1core + wqcopy + wqpass
    sent += g1xc + g2xc + g1last + g2last
    for copy in stores:
        copy.wait()
    for copy in sent:
        copy.wait_send()


def hand_over(a_ref, b_ref, c_ref, a_o, b_o, c_o, a_v, b_v, c_v, insem, outsem):
    moves = [(b_ref, b_v, b_o), (c_ref, c_v, c_o)]
    for k in range(4):
        rs = pl.ds(k * (N // 4), N // 4)
        moves.append((a_ref.at[rs, :], a_v.at[rs, :], a_o.at[rs, :]))
    taken = [pltpu.make_async_copy(m[0], m[1], insem.at[i]) for i, m in enumerate(moves)]
    given = [pltpu.make_async_copy(m[1], m[2], outsem.at[i]) for i, m in enumerate(moves)]
    for copy in taken:
        copy.start()
    for into, out in zip(taken, given):
        into.wait()
        out.start()
    for copy in given:
        copy.wait()


def shards(features, weight_in, weight_out, adj_tiles, tile_rows, tile_cols, tile_counts, cotangent):
    anyspace = pl.BlockSpec(memory_space=pl.ANY)
    V = pltpu.VMEM
    scratch = [
        pltpu.SMEM((5, 1, 8), jnp.int32), pltpu.SMEM((5, 1, 8), jnp.int32), pltpu.SMEM((1, 5), jnp.int32),
        V((N, W), BF), V((8, W), F32), V((8, W), F32),
        V((N, W), BF), V((2, 512, W), BF), V((2, 512, W), BF), V((5, 8, TILE, TILE), BF), V((N, W), BF),
        V((5, N, N), BF), V((4, N, W), BF), V((N, W), F32), V((2, N, W), BF), V((N, W), F32),
        V((2, N, W), BF), V((N, W), F32), V((N, W), F32), V((N, W), BF), V((N, W), BF), V((4, N, W), BF),
        V((4, N, W), BF), V((4, N, W), BF), V((N, W), F32), V((2, N, W), BF), V((2, N, W), BF),
        V((N, W), BF), V((N, W), F32), V((N - N * SPLIT // 8, W), BF), V((N - N * CSPLIT // 8, W), BF),
        V((NZ, NY, NX, NC, 8, W), F32), V((NZ, NY, NX, 8, W), F32), V((NZ, NY, NX, 16, W // 2), BF),
        V((3, NZ, NY, 16, W // 2), BF), V((NZ, NY, 16, W // 2), F32), V((NZ, NY, 16, W // 2), BF),
        V((15, 16, W // 2), BF),
        V((NZ, NY, NX, NC, 8, W), F32), V((NZ, NY, NX, 8, W), F32), V((NZ, NY, NX, 16, W // 2), BF),
        V((3, NZ, NY, 16, W // 2), BF), V((NZ, NY, 16, W // 2), F32), V((NZ, NY, 16, W // 2), BF),
        V((15, 16, W // 2), BF),
        pltpu.SemaphoreType.DMA((8 + 2 + N // SUB,)),
        pltpu.SemaphoreType.DMA((NREMOTE,)),
        pltpu.SemaphoreType.DMA((NREMOTE,)),
    ]
    results = pl.pallas_call(
        kernel,
        out_shape=(
            jax.ShapeDtypeStruct((N, W), BF),
            jax.ShapeDtypeStruct((8, W), F32),
            jax.ShapeDtypeStruct((8, W), F32),
        ),
        in_specs=[anyspace] * 8,
        out_specs=(anyspace,) * 3,
        scratch_shapes=scratch,
        compiler_params=pltpu.CompilerParams(
            collective_id=0, has_side_effects=True, vmem_limit_bytes=60 * 1024 * 1024
        ),
        name="graph_layers",
    )(
        features,
        weight_in.reshape(2, 512, W),
        weight_out.reshape(2, 512, W),
        adj_tiles.reshape(5, 8, TILE, TILE),
        tile_rows.transpose(1, 0, 2),
        tile_cols.transpose(1, 0, 2),
        tile_counts,
        cotangent,
    )
    return pl.pallas_call(
        hand_over,
        out_shape=tuple(jax.ShapeDtypeStruct(r.shape, r.dtype) for r in results),
        in_specs=[anyspace] * 3,
        out_specs=[anyspace] * 3,
        scratch_shapes=[
            V((N, W), BF), V((8, W), F32), V((8, W), F32),
            pltpu.SemaphoreType.DMA((6,)), pltpu.SemaphoreType.DMA((6,)),
        ],
        name="hand_over",
    )(*results)


def solution(mesh):
    return jax.shard_map(
        shards,
        mesh=mesh,
        in_specs=(
            P("blk", "feat"),
            P(None, "feat"),
            P(None, "feat"),
            P("blk", None, None, None, None),
            P("blk", None, None),
            P("blk", None, None),
            P("blk", None),
            P("blk", "feat"),
        ),
        out_specs=(P("blk", "feat"), P("blk", "feat"), P("blk", "feat")),
        check_vma=False,
    )
```

```python
import functools

import jax
import jax.numpy as jnp
from jax import lax
from jax.experimental import pallas as pl
from jax.experimental.pallas import tpu as pltpu
from jax.sharding import PartitionSpec as P

F32 = jnp.float32
BF = jnp.bfloat16
MESH = pl.DeviceIdType.MESH
NB = 128
NZ, NY, NX, NC = 8, 2, 4, 2
N = 512
W = 512
TILE = 128
XCH = 2
XW = W // XCH
RCH = 4
PWHEN = 0
SPLIT = 5
CSPLIT = 6
RW = N // RCH
SUB = 256


def dot(a, b):
    return jnp.dot(a, b, preferred_element_type=F32)


def dot_tn(a, b):
    return lax.dot_general(a, b, (((0,), (0,)), ((), ())), preferred_element_type=F32)


def dot_nt(a, b):
    return lax.dot_general(a, b, (((1,), (1,)), ((), ())), preferred_element_type=F32)


def fold(v):
    return jnp.concatenate([v[..., : W // 2], v[..., W // 2 :]], axis=-2)


def loop(count, body):
    def step(i, carry):
        body(i)
        return carry

    lax.fori_loop(0, count, step, 0)


def span(i, size):
    return pl.ds(pl.multiple_of(i * size, size), size)


class Sems:
    def __init__(self, send, recv):
        self.send, self.recv, self.used = send, recv, 0

    def make(self, src, dst, device):
        i = self.used
        self.used += 1
        return pltpu.make_async_remote_copy(
            src_ref=src,
            dst_ref=dst,
            send_sem=self.send.at[i],
            recv_sem=self.recv.at[i],
            device_id=device,
            device_id_type=MESH,
        )

    def choose(self, first, src, other, dst, device, other_device):
        made = self.make(src, dst, device)
        self.used -= 1
        turned = self.make(other, dst, other_device)
        pl.when(first)(lambda: made.start())
        pl.when(jnp.logical_not(first))(lambda: turned.start())
        return made

    def copy(self, src, dst, device):
        made = self.make(src, dst, device)
        made.start()
        return made


class Swap:
    def __init__(self, sems, edge, lo, hi, way, peer, turn, onward):
        self.edge = edge
        self.lo = sems.copy(lo[0], lo[1], peer)
        self.straight = sems.make(hi[0], hi[1], peer)
        self.out = sems.make(hi[0], way, turn)
        self.on = sems.make(way, hi[2], onward)
        self.pick(self.out.start, self.straight.start)

    def pick(self, at_edge, inside):
        pl.when(self.edge)(lambda: at_edge())
        pl.when(jnp.logical_not(self.edge))(lambda: inside())

    def pass_on(self):
        @pl.when(jnp.logical_not(self.edge))
        def _():
            self.out.wait_recv()
            self.on.start()

    def wait_recv(self):
        self.lo.wait_recv()
        self.pick(self.on.wait_recv, self.straight.wait_recv)

    def wait_send(self):
        self.lo.wait_send()

        def inside():
            self.straight.wait_send()
            self.on.wait_send()

        self.pick(self.out.wait_send, inside)


NREMOTE = 112


def kernel(
    x_h, win_h, wout_h, tiles_h, rows_h, cols_h, cnts_h, cot_h,
    out_h, gin_h, gout_h,
    rows, cols, cnts, out_o, gin_o, gout_o,
    x, win, wout, tiles, cot,
    a, xg, sacc, sfull, pre, hfull, dact, zacc, z, z2, zg,
    pbuf, pr, cacc, cfull, wq, bp, oacc, sway, cway,
    g1, g1c, g1r1, g1x, g1r2f, g1r2, g1l,
    g2, g2c, g2r1, g2x, g2r2f, g2r2, g2l,
    lsem, ssem, rsem,
):
    b = lax.axis_index("blk")
    f = lax.axis_index("feat")
    c = lax.rem(b, NC)
    ix = lax.rem(b // NC, NX)
    iy = lax.rem(b // (NC * NX), NY)
    iz = b // (NC * NX * NY)
    nf = 1 - f
    nc = 1 - c

    def node(zz, yy, xx, cc):
        return (((zz * NY + yy) * NX + xx) * NC + cc, f)

    def near(o):
        return (lax.rem(b + o + NB, NB), f)

    peer = (b, nf)
    edge = jnp.logical_or(ix == 0, ix == NX - 1)
    beside = ix + 1 - 2 * lax.rem(ix, 2)
    beside_node = (((iz * NY + iy) * NX + beside) * NC + c)
    turn, onward = (beside_node, nf), (beside_node, f)
    across = (((iz * NY + 1 - iy) * NX + ix) * NC + c, nf)
    partner = node(iz, iy, ix, nc)
    xpeers = [lax.rem(ix + d, NX) for d in (2, 1, 3)]
    zpeers = [lax.rem(iz + d, NZ) for d in (4, 3, 5, 2, 6, 1, 7)]
    ypeer = 1 - iy

    greeted = [near(2), near(-2), peer, partner, turn, across]
    greeted += [node(iz, iy, xx, c) for xx in xpeers]
    greeted += [node(zz, iy, ix, c) for zz in zpeers]
    greeted += [node(zz, ypeer, ix, c) for zz in [iz] + zpeers]

    barrier = pltpu.get_barrier_semaphore()
    for device in greeted:
        pl.semaphore_signal(barrier, inc=1, device_id=device, device_id_type=MESH)

    @pl.when(ix == 0)
    def _():
        pl.semaphore_signal(
            barrier, inc=1, device_id=(near(-2)[0], nf), device_id_type=MESH
        )

    @pl.when(ix == NX - 1)
    def _():
        pl.semaphore_signal(barrier, inc=1, device_id=(near(2)[0], nf), device_id_type=MESH)

    loads = []
    for i, (src, dst) in enumerate(
        ((x_h, x), (tiles_h, tiles), (cot_h, cot), (win_h, win), (wout_h, wout),
         (rows_h, rows), (cols_h, cols), (cnts_h, cnts))
    ):
        made = pltpu.make_async_copy(src, dst, lsem.at[i])
        made.start()
        loads.append(made)
    loads[0].wait()
    pl.semaphore_wait(barrier, len(greeted) + edge.astype(jnp.int32))

    sems = Sems(ssem, rsem)
    step_of = (0, 4, 3 - 2 * c, 1 + 2 * c)

    def swap(ref, out_slot, in_slot, start, size, cs, way, split):
        near_rows = size * split // 8
        lo, hi = pl.ds(start, near_rows), pl.ds(start + near_rows, size - near_rows)
        return Swap(
            sems, edge,
            (ref(out_slot, lo, cs), ref(in_slot[0], lo, cs)),
            (ref(out_slot, hi, cs), ref(in_slot[0], hi, cs), ref(in_slot[1], hi, cs)),
            way, peer, turn, onward,
        )

    def spread(src, dst):
        return [
            sems.copy(src, dst(0), near(2)),
            sems.copy(src, dst(1), near(-2)),
            sems.copy(src, dst(2), partner),
        ]

    def on_side(copies, side):
        @pl.when(side == 0)
        def _():
            copies[0].wait_recv()

        @pl.when(side == 1)
        def _():
            copies[1].wait_recv()

    xcopies = []
    for j in range(XCH):
        cs = pl.ds(j * XW, XW)
        xcopies.append(spread(x.at[:, cs], lambda i, cs=cs: xg.at[i, :, cs]))

    for i in (1, 5, 6, 7):
        loads[i].wait()

    def densify(s):
        live = cnts[0, s]
        place = [
            jnp.where(k < live, rows[s, 0, k] * 4 + cols[s, 0, k], -1) for k in range(8)
        ]
        for r in range(4):
            for q in range(4):
                block = jnp.zeros((TILE, TILE), BF)
                for k in range(8):
                    block = lax.select(place[k] == r * 4 + q, tiles[s, k], block)
                a[s, r * TILE : (r + 1) * TILE, q * TILE : (q + 1) * TILE] = block

    loop(5, densify)
    loads[2].wait()

    def own_s(i):
        sacc[span(i, SUB), :] = dot(a[2, span(i, SUB), :], x[...])

    loop(N // SUB, own_s)


    def product(slot, step, helped):
        def rows_of(k):
            rs = span(k, SUB)
            part = dot_tn(a[step, :, rs], cot[...])
            if helped:
                part += pr[3, rs, :].astype(F32)
            pbuf[slot, rs, :] = part.astype(BF)

        loop(N // SUB, rows_of)

    product(2, step_of[2], False)
    pcopies = [sems.copy(pbuf.at[2], pr.at[2], partner)]
    product(3, step_of[3], False)
    help_copy = sems.copy(pbuf.at[3], pr.at[3], partner)
    product(c, 4 * c, False)

    def own_c(k):
        cacc[span(k, SUB), :] = dot_tn(a[2, :, span(k, SUB)], cot[...])

    loop(N // SUB, own_c)
    help_copy.wait_recv()
    product(nc, 4 * nc, True)

    def send_products():
        pcopies.append(sems.copy(pbuf.at[c], pr.at[c], near(4 * c - 2)))
        pcopies.append(sems.copy(pbuf.at[nc], pr.at[nc], near(4 * nc - 2)))

    if PWHEN == 0:
        send_products()
    scopies = []
    relays = []
    for j in range(XCH):
        cs = pl.ds(j * XW, XW)

        def add(i, last=False):
            def rows_of(k):
                rs = span(k, SUB)
                total = sacc[rs, cs] + dot(a[step_of[i], rs, :], xg[i, :, cs])
                if last:
                    sfull[f, rs, cs] = total.astype(BF)
                else:
                    sacc[rs, cs] = total

            loop(N // SUB, rows_of)

        xcopies[j][2].wait_recv()
        add(2)
        on_side(xcopies[j], nc)
        relay = sems.copy(xg.at[nc, :, cs], xg.at[3, :, cs], partner)
        relays.append(relay)
        on_side(xcopies[j], c)
        add(0)
        add(1)
        relay.wait_recv()
        add(3, True)
        scopies.append(
            swap(lambda i, r, q: sfull.at[i, r, q], f, (f, nf), 0, N, cs, sway.at[:, cs], SPLIT)
        )
    if PWHEN == 1:
        send_products()

    loads[4].wait()
    half = pl.ds(pl.multiple_of(c * (N // 2), N // 2), N // 2)
    wqcopy = [
        sems.copy(wout.at[nf, half, :], wq.at[0, half, :], across),
        sems.copy(wout.at[f, half, :], wq.at[1, half, :], across),
    ]
    loads[3].wait()

    def pre_own(k):
        rs = span(k, SUB)
        pre[rs, :] = dot(sfull[f, rs, :], win[f])

    loop(N // SUB, pre_own)
    for j in range(XCH - 1):
        cs = pl.ds(j * XW, XW)
        scopies[j].pass_on()
        scopies[j].wait_recv()

        def pre_add(k):
            rs = span(k, SUB)
            pre[rs, :] += dot(sfull[nf, rs, cs], win[nf, cs, :])

        loop(N // SUB, pre_add)
    cs = pl.ds((XCH - 1) * XW, XW)
    scopies[-1].pass_on()
    scopies[-1].wait_recv()
    if PWHEN == 2:
        send_products()
    hcopies = []

    def hidden_piece(j):

        def act(k):
            rs = pl.ds(pl.multiple_of(j * RW + k * TILE, TILE), TILE)
            v = pre[rs, :] + dot(sfull[nf, rs, cs], win[nf, cs, :])
            g = 1.0 / (1.0 + jnp.exp(-v))
            hfull[f, rs, :] = (v * g).astype(BF)
            dact[rs, :] = g * (1.0 + v * (1.0 - g))

        loop(RW // TILE, act)
        rs = pl.ds(j * RW, RW)
        hcopies.append(sems.copy(hfull.at[f, rs, :], hfull.at[f, rs, :], peer))

    hidden_piece(0)
    hidden_piece(1)
    hidden_piece(2)
    hidden_piece(3)
    for copy in pcopies:
        copy.wait_recv()

    def close_c(k):
        rs = span(k, TILE)
        total = cacc[rs, :]
        for i in range(3):
            total += pr[i, rs, :].astype(F32)
        cfull[f, rs, :] = total.astype(BF)

    loop(N // TILE, close_c)

    ccopy = swap(
        lambda i, r, q: cfull.at[i, r, q], f, (f, nf), 0, N, pl.ds(0, W), cway, CSPLIT
    )

    def z_own(k):
        rs = span(k, SUB)
        zacc[rs, :] = dot(hfull[f, rs, :], wout[f])

    loop(N // SUB, z_own)
    wqpass = []
    for i in range(2):
        wqcopy[i].wait_recv()
        wqpass.append(sems.copy(wq.at[i, half, :], wq.at[i, half, :], partner))


    def gout_rows(side):
        def rows_of(k):
            part = dot_tn(hfull[side, :, span(k, TILE)], cfull[f])
            g1[side * 4 + k] = part.reshape(NY, NX, NC, 8, W)

        loop(4, rows_of)

    def side_of(ref, side, *rest):
        return ref.at[(pl.ds(side * 4, 4), *rest)]

    def to_partner(g, gc, side):
        return sems.copy(
            side_of(g, side, slice(None), slice(None), nc), side_of(gc, side), partner
        )

    def across_x(copy, g, gc, r1, gx, side):
        copy.wait_recv()

        def first(k):
            i = side * 4 + k
            r1[i] = fold(g[i, :, :, c] + gc[i]).astype(BF)

        loop(4, first)
        return [
            sems.copy(
                side_of(r1, side, slice(None), xx), gx.at[d, pl.ds(side * 4, 4)],
                node(iz, iy, xx, c),
            )
            for d, xx in enumerate(xpeers)
        ]

    gout_rows(f)
    g1core = [to_partner(g1, g1c, f)]

    def bh_own(k):
        rs = span(k, SUB)
        cacc[rs, :] = dot_nt(cfull[f, rs, :], wout[f])

    loop(N // SUB, bh_own)
    for copy in wqpass:
        copy.wait_recv()
    g1xc = across_x(g1core[0], g1, g1c, g1r1, g1x, f)
    zcopies = []

    def z_piece(j):
        hcopies[j].wait_recv()
        rs = pl.ds(j * RW, RW)
        z[rs, :] = (zacc[rs, :] + dot(hfull[nf, rs, :], wout[nf])).astype(BF)

        @pl.when(edge)
        def _():
            z2[rs, :] = (
                dot(hfull[f, rs, :], wq[0]) + dot(hfull[nf, rs, :], wq[1])
            ).astype(BF)

        mine, turned = z.at[rs, :], z2.at[rs, :]
        zcopies.append([
            sems.choose(ix != NX - 1, mine, turned, zg.at[0, rs, :], near(2), (near(2)[0], nf)),
            sems.choose(ix != 0, mine, turned, zg.at[1, rs, :], near(-2), (near(-2)[0], nf)),
            sems.copy(mine, zg.at[2, rs, :], partner),
        ])

    z_piece(0)
    z_piece(1)
    z_piece(2)
    z_piece(3)
    gout_rows(nf)
    g1core.append(to_partner(g1, g1c, nf))
    def own_o(k):
        rs = span(k, SUB)
        oacc[rs, :] = dot(a[2, rs, :], z[...])

    loop(N // SUB, own_o)
    g1xc += across_x(g1core[1], g1, g1c, g1r1, g1x, nf)

    def second(g, gc, gx, r2f, r2):
        def part(k):
            total = fold(g[k, :, ix, c] + gc[k, :, ix])
            for d in range(NX - 1):
                total += gx[d, k].astype(F32)
            r2f[k] = total
            r2[k] = total.astype(BF)

        loop(NZ, part)

    stores = []

    def relay_part(part):
        made = []
        for j in range(part * RCH // 2, (part + 1) * RCH // 2):
            ks = pl.ds(j * RW, RW)
            on_side(zcopies[j], nc)
            made.append(sems.copy(zg.at[nc, ks, :], zg.at[3, ks, :], partner))
            zcopies[j][2].wait_recv()
            on_side(zcopies[j], c)
        relays.extend(made)
        return made

    def out_part(made, part):
        ks = pl.ds(part * (N // 2), N // 2)

        def direct(k):
            rs = span(k, SUB)
            total = oacc[rs, :]
            for i in range(3):
                total += dot(a[step_of[i], rs, ks], zg[i, ks, :])
            oacc[rs, :] = total

        loop(N // SUB, direct)
        for copy in made:
            copy.wait_recv()
        for k in range(N // SUB):
            rs = pl.ds(k * SUB, SUB)
            total = oacc[rs, :] + dot(a[step_of[3], rs, ks], zg[3, ks, :])
            if part == 0:
                oacc[rs, :] = total
            else:
                out_o[rs, :] = total.astype(BF)
                stores.append(
                    pltpu.make_async_copy(out_o.at[rs, :], out_h.at[rs, :], lsem.at[10 + k])
                )
                stores[-1].start()


    far = [(zz, yy) for zz in zpeers for yy in (ypeer, iy)] + [(iz, ypeer)]

    def second(g, gc, gx, r2f, r2):
        def part(k):
            total = fold(g[k, :, ix, c] + gc[k, :, ix])
            for d in range(NX - 1):
                total += gx[d, k].astype(F32)
            r2f[k] = total
            r2[k] = total.astype(BF)

        loop(NZ, part)

    stores = []

    def relay_part(part):
        made = []
        for j in range(part * RCH // 2, (part + 1) * RCH // 2):
            ks = pl.ds(j * RW, RW)
            on_side(zcopies[j], nc)
            made.append(sems.copy(zg.at[nc, ks, :], zg.at[3, ks, :], partner))
            zcopies[j][2].wait_recv()
            on_side(zcopies[j], c)
        relays.extend(made)
        return made

    def out_part(made, part):
        ks = pl.ds(part * (N // 2), N // 2)

        def direct(k):
            rs = span(k, SUB)
            total = oacc[rs, :]
            for i in range(3):
                total += dot(a[step_of[i], rs, ks], zg[i, ks, :])
            oacc[rs, :] = total

        loop(N // SUB, direct)
        for copy in made:
            copy.wait_recv()
        for k in range(N // SUB):
            rs = pl.ds(k * SUB, SUB)
            total = oacc[rs, :] + dot(a[step_of[3], rs, ks], zg[3, ks, :])
            if part == 0:
                oacc[rs, :] = total
            else:
                out_o[rs, :] = total.astype(BF)
                stores.append(
                    pltpu.make_async_copy(out_o.at[rs, :], out_h.at[rs, :], lsem.at[10 + k])
                )
                stores[-1].start()


    far = [
        (zz, yy) for zz in [iz] + zpeers for yy in (iy, ypeer)
    ][1:]

    def second(copies, g, gc, gx, r2f, r2, gl):
        for copy in copies:
            copy.wait_recv()

        def part(k):
            total = fold(g[k, :, ix, c] + gc[k, :, ix])
            for d in range(NX - 1):
                total += gx[d, k].astype(F32)
            r2f[k] = total
            r2[k] = total.astype(BF)

        loop(NZ, part)
        return [
            sems.copy(r2.at[zz, yy], gl.at[d], node(zz, yy, ix, c))
            for d, (zz, yy) in enumerate(far)
        ]

    def last(copies, r2f, gl, to, into, i):
        for copy in copies:
            copy.wait_recv()
        total = r2f[iz, iy]
        for d in range(len(far)):
            total += gl[d].astype(F32)
        to[:, : W // 2] = total[:8]
        to[:, W // 2 :] = total[8:]
        stores.append(pltpu.make_async_copy(to, into, lsem.at[i]))
        stores[-1].start()

    ccopy.pass_on()
    part0 = relay_part(0)
    out_part(part0, 0)
    ccopy.wait_recv()

    def close_bp(k):
        rs = span(k, SUB)
        back = cacc[rs, :] + dot_nt(cfull[nf, rs, :], wq[0])
        bp[rs, :] = (back * dact[rs, :]).astype(BF)

    loop(N // SUB, close_bp)
    g2core = []
    for side in range(2):

        def gin_rows(k, side=side):
            part = dot_tn(sfull[side, :, span(k, TILE)], bp[...])
            g2[side * 4 + k] = part.reshape(NY, NX, NC, 8, W)

        loop(4, gin_rows)
        g2core.append(to_partner(g2, g2c, side))
    g2xc = []
    for side in range(2):
        g2xc += across_x(g2core[side], g2, g2c, g2r1, g2x, side)
    g1last = second(g1xc, g1, g1c, g1x, g1r2f, g1r2, g1l)
    part1 = relay_part(1)
    out_part(part1, 1)
    g2last = second(g2xc, g2, g2c, g2x, g2r2f, g2r2, g2l)
    last(g1last, g1r2f, g1l, gout_o, gout_h, 9)
    last(g2last, g2r2f, g2l, gin_o, gin_h, 8)

    sent = [copy for group in xcopies + zcopies for copy in group] + pcopies + scopies + hcopies + relays
    sent += [help_copy, ccopy] + g2core + g1core + wqcopy + wqpass
    sent += g1xc + g2xc + g1last + g2last
    for copy in stores:
        copy.wait()
    for copy in sent:
        copy.wait_send()


def hand_over(a_ref, b_ref, c_ref, a_o, b_o, c_o, a_v, b_v, c_v, insem, outsem):
    moves = [(b_ref, b_v, b_o), (c_ref, c_v, c_o)]
    for k in range(4):
        rs = pl.ds(k * (N // 4), N // 4)
        moves.append((a_ref.at[rs, :], a_v.at[rs, :], a_o.at[rs, :]))
    taken = [pltpu.make_async_copy(m[0], m[1], insem.at[i]) for i, m in enumerate(moves)]
    given = [pltpu.make_async_copy(m[1], m[2], outsem.at[i]) for i, m in enumerate(moves)]
    for copy in taken:
        copy.start()
    for into, out in zip(taken, given):
        into.wait()
        out.start()
    for copy in given:
        copy.wait()


def shards(features, weight_in, weight_out, adj_tiles, tile_rows, tile_cols, tile_counts, cotangent):
    anyspace = pl.BlockSpec(memory_space=pl.ANY)
    V = pltpu.VMEM
    scratch = [
        pltpu.SMEM((5, 1, 8), jnp.int32), pltpu.SMEM((5, 1, 8), jnp.int32), pltpu.SMEM((1, 5), jnp.int32),
        V((N, W), BF), V((8, W), F32), V((8, W), F32),
        V((N, W), BF), V((2, 512, W), BF), V((2, 512, W), BF), V((5, 8, TILE, TILE), BF), V((N, W), BF),
        V((5, N, N), BF), V((4, N, W), BF), V((N, W), F32), V((2, N, W), BF), V((N, W), F32),
        V((2, N, W), BF), V((N, W), F32), V((N, W), F32), V((N, W), BF), V((N, W), BF), V((4, N, W), BF),
        V((4, N, W), BF), V((4, N, W), BF), V((N, W), F32), V((2, N, W), BF), V((2, N, W), BF),
        V((N, W), BF), V((N, W), F32), V((N - N * SPLIT // 8, W), BF), V((N - N * CSPLIT // 8, W), BF),
        V((NZ, NY, NX, NC, 8, W), F32), V((NZ, NY, NX, 8, W), F32), V((NZ, NY, NX, 16, W // 2), BF),
        V((3, NZ, NY, 16, W // 2), BF), V((NZ, NY, 16, W // 2), F32), V((NZ, NY, 16, W // 2), BF),
        V((15, 16, W // 2), BF),
        V((NZ, NY, NX, NC, 8, W), F32), V((NZ, NY, NX, 8, W), F32), V((NZ, NY, NX, 16, W // 2), BF),
        V((3, NZ, NY, 16, W // 2), BF), V((NZ, NY, 16, W // 2), F32), V((NZ, NY, 16, W // 2), BF),
        V((15, 16, W // 2), BF),
        pltpu.SemaphoreType.DMA((8 + 2 + N // SUB,)),
        pltpu.SemaphoreType.DMA((NREMOTE,)),
        pltpu.SemaphoreType.DMA((NREMOTE,)),
    ]
    results = pl.pallas_call(
        kernel,
        out_shape=(
            jax.ShapeDtypeStruct((N, W), BF),
            jax.ShapeDtypeStruct((8, W), F32),
            jax.ShapeDtypeStruct((8, W), F32),
        ),
        in_specs=[anyspace] * 8,
        out_specs=(anyspace,) * 3,
        scratch_shapes=scratch,
        compiler_params=pltpu.CompilerParams(
            collective_id=0, has_side_effects=True, vmem_limit_bytes=60 * 1024 * 1024
        ),
        name="graph_layers",
    )(
        features,
        weight_in.reshape(2, 512, W),
        weight_out.reshape(2, 512, W),
        adj_tiles.reshape(5, 8, TILE, TILE),
        tile_rows.transpose(1, 0, 2),
        tile_cols.transpose(1, 0, 2),
        tile_counts,
        cotangent,
    )
    return pl.pallas_call(
        hand_over,
        out_shape=tuple(jax.ShapeDtypeStruct(r.shape, r.dtype) for r in results),
        in_specs=[anyspace] * 3,
        out_specs=[anyspace] * 3,
        scratch_shapes=[
            V((N, W), BF), V((8, W), F32), V((8, W), F32),
            pltpu.SemaphoreType.DMA((6,)), pltpu.SemaphoreType.DMA((6,)),
        ],
        name="hand_over",
    )(*results)


def solution(mesh):
    return jax.shard_map(
        shards,
        mesh=mesh,
        in_specs=(
            P("blk", "feat"),
            P(None, "feat"),
            P(None, "feat"),
            P("blk", None, None, None, None),
            P("blk", None, None),
            P("blk", None, None),
            P("blk", None),
            P("blk", "feat"),
        ),
        out_specs=(P("blk", "feat"), P("blk", "feat"), P("blk", "feat")),
        check_vma=False,
    )
```
